128 devices in a mesh: slab: 16 (over y, x_lo, core), head: 8 (over z, x_hi).
Axes of the slice: x: 4 (x_hi: 2, x_lo: 2; x = x_hi * 2 + x_lo), y: 4, z: 4, core: 2. Of those that a mesh axis runs over, the one named last changes fastest.
Arguments:
- hidden_states: bfloat16 [6144, 6144], P(('slab', 'head')), may hold values from -36 to 36
- qkv_weight: bfloat16 [3, 6144, 3072], P(None, None, 'head'), may hold values from -0.078125 to 0.078125
- out_grad: bfloat16 [6144, 3072], P('slab', 'head'), may hold values from -6 to 6
- tile_frame: int32 [48], replicated, may hold values from 0 to 2, as said below
- frame_band: int32 [24], P('head'), may hold values from 0 to 2
Outputs:
- attn_out: bfloat16 [6144, 3072], P('slab', 'head')
- grad_hidden: bfloat16 [6144, 6144], P(('slab', 'head'))
The draws below stay inside these ranges and needn't reach their ends.
Inputs may be any that keep to these rules, and one draw needn't show every extreme that they name: `tile_frame`: the tiles of one frame are consecutive; tile 0 lies in frame 0, each tile lies in the frame of the tile before it or in the next one, and the last tile lies in frame 2.
All inputs are finite; a program needn't handle non-finite values.
Results may differ from the reference program's by a relative error of at most 0.03.
The reference program's roundings to bfloat16 on the way count: a program that leaves them out, or rounds other values in their place, can miss the bound.
Values may be sent and summed in bfloat16 or wider, within the bound.
No kernel may reach another device: no remote copies, remote signals or barrier semaphores. Data moves between devices by JAX's collectives and lax.ppermute only.
A program may use at most 192 MiB of HBM per device.

```python
import math
import jax
import jax.numpy as jnp
from jax import lax

D = 6144
DH = 128
TILE = 128
FRAMES = 3
HEADS = 24
NT = 48
TOKENS = 6144


def draw_hidden_states(key, part):
    first = jax.random.fold_in(key, 0)
    values = jnp.clip(jax.random.normal(first, (TOKENS, D), jnp.float32), -6.0, 6.0)
    return values.astype(jnp.bfloat16)


def draw_tile_frame(key, part):
    span_tiles = NT // FRAMES
    quarter = NT // (4 * FRAMES)
    jitter = jax.random.randint(key, (FRAMES - 1,), -quarter, quarter + 1)
    bounds = jnp.arange(1, FRAMES, dtype=jnp.int32) * span_tiles + jitter
    tiles = jnp.arange(NT, dtype=jnp.int32)
    return jnp.sum((tiles[:, None] >= bounds[None, :]).astype(jnp.int32), axis=1).astype(jnp.int32)


def place_ends(array, key, smallest, largest):
    longest = array.shape.index(max(array.shape))
    spots = []
    for shift in (0, 1):
        where = [jax.random.randint(jax.random.fold_in(key, axis), (), 0, length) for axis, length in enumerate(array.shape)]
        where[longest] = (where[longest] + shift) % array.shape[longest]
        spots.append(tuple(where))
    return array.at[spots[0]].set(smallest).at[spots[1]].set(largest)


def block_levels(stream_key, extent, pieces, smallest, high):
    def one(position, shards_of):
        steps = jax.random.uniform(jax.random.fold_in(jax.random.fold_in(stream_key, 6), position), (shards_of,), jnp.float32, smallest / len(pieces), high / len(pieces))
        return jnp.repeat(jnp.exp(steps), extent[position] // shards_of).reshape((-1,) + (1,) * (len(extent) - position - 1))

    factor_of = one(*pieces[0])
    for cut in pieces[1:]:
        factor_of = factor_of * one(*cut)
    return factor_of


def scatter_about(key, extent, scale, limit, cuts=(), kind=jnp.bfloat16):
    factor_of = block_levels(key, extent, cuts, -0.22, 0.18) if cuts else 1.0
    result = jax.random.normal(key, extent, jnp.float32) * scale * factor_of
    return jnp.minimum(jnp.maximum(result, -limit), limit).astype(kind)


def setup_inputs(seed: int = 0) -> dict:
    key_list = jax.random.split(jax.random.key(seed), 6)
    hidden_states = draw_hidden_states(jax.random.fold_in(key_list[5], 71), 0)
    qkv_weight = scatter_about(key_list[1], (3, D, HEADS * DH), D ** -0.5, 0.078125, ((2, 8),))
    out_grad = scatter_about(key_list[2], (TOKENS, HEADS * DH), 1.0, 6.0, ((0, 16), (1, 8)))
    tile_frame = draw_tile_frame(jax.random.fold_in(key_list[5], 71), 0)
    frame_band = place_ends(jax.random.randint(key_list[4], (HEADS,), 0, FRAMES), jax.random.fold_in(key_list[4], 1), 0, FRAMES - 1).astype(jnp.int32)
    return dict(hidden_states=hidden_states, qkv_weight=qkv_weight, out_grad=out_grad, tile_frame=tile_frame, frame_band=frame_band)


def reference(hidden_states, qkv_weight, out_grad, tile_frame, frame_band):
    factor = 1.0 / math.sqrt(DH)
    projected = [jnp.dot(hidden_states, qkv_weight[c], preferred_element_type=jnp.float32).astype(jnp.bfloat16) for c in range(3)]
    frames = jnp.repeat(tile_frame, TILE)

    def by_head(matrix):
        return matrix.reshape(TOKENS, HEADS, DH).transpose(1, 0, 2)

    def one_head(packed):
        queries, keys, values, grad_part, reach = packed
        scores = jnp.dot(queries, keys.T, preferred_element_type=jnp.float32) * factor
        inside = jnp.abs(frames[:, None] - frames[None, :]) <= reach
        masked = jnp.where(inside, scores, -1e+30)
        peak = lax.optimization_barrier(jnp.max(masked, axis=1))
        weights = jnp.where(inside, jnp.exp(masked - peak[:, None]), 0.0)
        weight_sum = lax.optimization_barrier(jnp.sum(weights, axis=1))
        output = (jnp.dot(weights.astype(jnp.bfloat16), values, preferred_element_type=jnp.float32) / weight_sum[:, None]).astype(jnp.bfloat16)
        log_total = peak + jnp.log(weight_sum)
        row_delta = lax.optimization_barrier(jnp.sum(grad_part.astype(jnp.float32) * output.astype(jnp.float32), axis=1))
        probabilities = jnp.where(inside, jnp.exp(masked - log_total[:, None]), 0.0)
        value_grad = jnp.dot(probabilities.astype(jnp.bfloat16).T, grad_part, preferred_element_type=jnp.float32)
        grad_probs = jnp.dot(grad_part, values.T, preferred_element_type=jnp.float32)
        grad_scores = (probabilities * (grad_probs - row_delta[:, None])).astype(jnp.bfloat16)
        query_grad = jnp.dot(grad_scores, keys, preferred_element_type=jnp.float32) * factor
        key_grad = jnp.dot(grad_scores.T, queries, preferred_element_type=jnp.float32) * factor
        return (output, query_grad.astype(jnp.bfloat16), key_grad.astype(jnp.bfloat16), value_grad.astype(jnp.bfloat16))
    results = lax.map(one_head, (by_head(projected[0]), by_head(projected[1]), by_head(projected[2]), by_head(out_grad), frame_band))

    def by_token(stacked):
        return stacked.transpose(1, 0, 2).reshape(TOKENS, HEADS * DH)
    attn_out = by_token(results[0])
    grad_total = jnp.dot(by_token(results[1]), qkv_weight[0].T, preferred_element_type=jnp.float32)
    grad_total = grad_total + jnp.dot(by_token(results[2]), qkv_weight[1].T, preferred_element_type=jnp.float32)
    grad_total = grad_total + jnp.dot(by_token(results[3]), qkv_weight[2].T, preferred_element_type=jnp.float32)
    return (attn_out, grad_total.astype(jnp.bfloat16))
```

```python
import functools
import math

import jax
import jax.numpy as jnp
from jax import lax
from jax.experimental import pallas as pl
from jax.experimental.pallas import tpu as pltpu
from jax.sharding import PartitionSpec as P

TILE = 128
BF = jnp.bfloat16
F32 = jnp.float32
NT_DIMS = (((1,), (1,)), ((), ()))
FAR = 1e30
FROM = ((0, 1, 2, 3), (2, 0, 3, 1), (1, 3, 0, 2), (3, 2, 1, 0))
STEPS = (0, -1, 1, 2)


def params():
    return pltpu.CompilerParams(vmem_limit_bytes=60 * 1024 * 1024)


def dot(a, b):
    return jnp.dot(a, b, preferred_element_type=F32)


def dot_nt(a, b):
    return lax.dot_general(a, b, NT_DIMS, preferred_element_type=F32)


def project_kernel(last, place, *refs):
    blocks, (w_ref, acc_in), outs, (rows, acc) = refs[:8], refs[8:10], refs[10:-2], refs[-2:]
    step = pl.program_id(0)

    @pl.when(step == 0)
    def _():
        if acc_in is None:
            acc[...] = jnp.zeros_like(acc)
        else:
            acc[...] = acc_in[...]

    height = blocks[0].shape[0]
    for i, block in enumerate(blocks):
        rows[pl.ds(pl.multiple_of(place[i] * height, 16), height), :] = block[...]
    x = rows[...]
    for c in range(3):
        acc[c] += dot(x, w_ref[c])

    @pl.when(step == pl.num_programs(0) - 1)
    def _():
        if last:
            q_ref, kv_ref = outs
            width = acc.shape[2]
            q_ref[...] = acc[0].astype(BF)
            kv_ref[:, :width] = acc[1].astype(BF)
            kv_ref[:, width:] = acc[2].astype(BF)
        else:
            outs[0][...] = acc[...]


def project(place, blocks, weight, half, acc=None, chunk=512):
    height, columns = blocks[0].shape
    width = weight.shape[2]
    total = 8 * height
    steps = columns // chunk
    block_spec = pl.BlockSpec((height, chunk), lambda k, place: (0, k))
    w_spec = pl.BlockSpec((3, chunk, width), lambda k, place: (0, k + half * steps, 0))
    acc_shape = jax.ShapeDtypeStruct((3, total, width), F32)
    whole = pl.BlockSpec((3, total, width), lambda k, place: (0, 0, 0))
    if acc is None:
        body = lambda place, *refs: project_kernel(False, place, *refs[:9], None, *refs[9:])
        ins, extra, out_shape, out_specs = [], [], acc_shape, whole
    else:
        body = functools.partial(project_kernel, True)
        ins, extra = [acc], [whole]
        out_shape = (
            jax.ShapeDtypeStruct((total, width), BF),
            jax.ShapeDtypeStruct((total, 2 * width), BF),
        )
        out_specs = (
            pl.BlockSpec((total, width), lambda k, place: (0, 0)),
            pl.BlockSpec((total, 2 * width), lambda k, place: (0, 0)),
        )
    return pl.pallas_call(
        body,
        out_shape=out_shape,
        grid_spec=pltpu.PrefetchScalarGridSpec(
            num_scalar_prefetch=1,
            grid=(steps,),
            in_specs=[block_spec] * 8 + [w_spec] + extra,
            out_specs=out_specs,
            scratch_shapes=[pltpu.VMEM((total, chunk), BF), pltpu.VMEM((3, total, width), F32)],
        ),
        compiler_params=params(),
        name="project",
    )(place, *blocks, weight, *ins)


def forward_kernel(scale2, q0, q1, q2, q3, g0, g1, g2, g3, kv0, kv1, kv2, kv3, bias, ot, stat, qs, gt, kv, vt):
    size, width = q0.shape
    heads = width // TILE
    for b, (q, g, k) in enumerate(((q0, g0, kv0), (q1, g1, kv1), (q2, g2, kv2), (q3, g3, kv3))):
        qs[b] = q[...]
        kv[b * size : (b + 1) * size, :] = k[:, :width]
        for h in range(heads):
            at = slice(h * TILE, (h + 1) * TILE)
            gt[b, h] = g[:, at].T
            vt[h, :, b * size : (b + 1) * size] = k[:, width + h * TILE : width + (h + 1) * TILE].T
    tiles = kv.shape[0] // TILE

    def step(b, carry):
        for h in range(heads):
            at = slice(h * TILE, (h + 1) * TILE)
            s = dot_nt(kv[:, at], qs[b, :, at])
            away = bias[b, h]
            peak = jnp.full((1, size), -FAR, F32)
            for t in range(tiles):
                top = jnp.max(s[t * TILE : (t + 1) * TILE], axis=0, keepdims=True) * scale2
                peak = jnp.maximum(peak, top + away[t : t + 1])
            total = jnp.zeros((1, size), F32)
            parts = []
            for t in range(tiles):
                base = jnp.where(away[t : t + 1] < 0, FAR, peak)
                p = jnp.exp2(s[t * TILE : (t + 1) * TILE] * scale2 - base)
                total = total + jnp.sum(p, axis=0, keepdims=True)
                parts.append(p.astype(BF))
            o = dot(vt[h], jnp.concatenate(parts, axis=0))
            stat[b, 3 * h : 3 * h + 1, :] = peak
            stat[b, 3 * h + 1 : 3 * h + 2, :] = total
            stat[b, 3 * h + 2 : 3 * h + 3, :] = jnp.sum(o * gt[b, h].astype(F32), axis=0, keepdims=True)
            ot[b, h] = (o * jnp.where(total > 0, 1.0 / total, 0.0)).astype(BF)
        return carry

    lax.fori_loop(0, 4, step, 0)


def forward(scale2, queries, grads, pairs, bias):
    size, width = queries[0].shape
    heads = width // TILE
    return pl.pallas_call(
        functools.partial(forward_kernel, scale2),
        out_shape=(
            jax.ShapeDtypeStruct((4, heads, TILE, size), BF),
            jax.ShapeDtypeStruct((4, 3 * heads, size), F32),
        ),
        scratch_shapes=[
            pltpu.VMEM((4, size, width), BF),
            pltpu.VMEM((4, heads, TILE, size), BF),
            pltpu.VMEM((4 * size, width), BF),
            pltpu.VMEM((heads, TILE, 4 * size), BF),
        ],
        compiler_params=params(),
        name="forward",
    )(*queries, *grads, *pairs, bias)


def totals_kernel(s0, s1, s2, s3, lse_ref, delta_ref):
    heads = lse_ref.shape[1]
    sources = (s0, s1, s2, s3)
    for p in range(4):
        for h in range(heads):
            rows = [
                [s[FROM[j][p], 3 * h + i : 3 * h + i + 1, :] for i in range(3)]
                for j, s in enumerate(sources)
            ]
            peak = functools.reduce(jnp.maximum, [r[0] for r in rows])
            shrink = [jnp.exp2(r[0] - peak) for r in rows]
            total = sum(r[1] * f for r, f in zip(rows, shrink))
            lse_ref[p, h : h + 1, :] = peak + jnp.log2(total)
            delta_ref[p, h : h + 1, :] = sum(r[2] * f for r, f in zip(rows, shrink)) / total


def totals(stats):
    _, rows, size = stats[0].shape
    shape = jax.ShapeDtypeStruct((4, rows // 3, size), F32)
    return pl.pallas_call(totals_kernel, out_shape=(shape, shape), compiler_params=params(), name="totals")(*stats)


def merge_kernel(o0, o1, o2, o3, s0, s1, s2, s3, out):
    heads = o0.shape[0]
    for h in range(heads):
        rows = [
            [s[FROM[j][0], 3 * h + i : 3 * h + i + 1, :] for i in range(2)]
            for j, s in enumerate((s0, s1, s2, s3))
        ]
        peak = functools.reduce(jnp.maximum, [r[0] for r in rows])
        shares = [r[1] * jnp.exp2(r[0] - peak) for r in rows]
        whole = sum(shares)
        o = sum(x[h].astype(F32) * (share / whole) for x, share in zip((o0, o1, o2, o3), shares))
        out[:, h * TILE : (h + 1) * TILE] = o.T.astype(BF)


def merge(outs, stats):
    heads, _, size = outs[0].shape
    return pl.pallas_call(
        merge_kernel,
        out_shape=jax.ShapeDtypeStruct((size, heads * TILE), BF),
        compiler_params=params(),
        name="merge",
    )(*outs, *stats)


def backward_kernel(scale2, factor, first, *refs):
    q_refs, g_refs, (kv_a, kv_b, lse, delta, bias) = refs[:4], refs[4:8], refs[8:13]
    rest = refs[13:]
    if first:
        dq_in, (dkv_a, dkv_b, dq_out) = None, rest[:3]
    else:
        dq_in, (dkv_a, dkv_b, dq_out) = rest[0], rest[1:4]
    qs, gs, ks, vs, kt, dk, dv = rest[-7:]
    size, width = q_refs[0].shape
    heads = width // TILE
    for b in range(4):
        qs[b] = q_refs[b][...]
        gs[b] = g_refs[b][...]
    for i, k in enumerate((kv_a, kv_b)):
        ks[i * size : (i + 1) * size, :] = k[:, :width]
        vs[i * size : (i + 1) * size, :] = k[:, width:]
        for h in range(heads):
            kt[h, :, i * size : (i + 1) * size] = k[:, h * TILE : (h + 1) * TILE].T
    dk[...] = jnp.zeros_like(dk)
    dv[...] = jnp.zeros_like(dv)
    tiles = 2 * size // TILE

    def step(b, carry):
        for h in range(heads):
            at = slice(h * TILE, (h + 1) * TILE)
            q, g = qs[b, :, at], gs[b, :, at]
            s = dot_nt(ks[:, at], q)
            dp = dot_nt(vs[:, at], g)
            away, top, shift = bias[b, h], lse[b, h : h + 1], delta[b, h : h + 1]
            probs, grads = [], []
            for t in range(tiles):
                rows = slice(t * TILE, (t + 1) * TILE)
                base = jnp.where(away[t : t + 1] < 0, FAR, top)
                p = jnp.exp2(s[rows] * scale2 - base)
                probs.append(p.astype(BF))
                grads.append((p * (dp[rows] - shift)).astype(BF))
            p = jnp.concatenate(probs, axis=0)
            ds = jnp.concatenate(grads, axis=0)
            dv[:, at] += dot(p, g)
            dk[:, at] += dot(ds, q)
            dq = dot(kt[h], ds)
            if first:
                dq_out[b, h] = dq
            else:
                dq_out[b, :, at] = ((dq_in[b, h] + dq) * factor).T.astype(BF)
        return carry

    lax.fori_loop(0, 4, step, 0)
    for i, out in enumerate((dkv_a, dkv_b)):
        rows = slice(i * size, (i + 1) * size)
        out[:, :width] = (dk[rows] * factor).astype(BF)
        out[:, width:] = dv[rows].astype(BF)


def backward(scale2, factor, queries, grads, pairs, lse, delta, bias, dq=None):
    size, width = queries[0].shape
    heads = width // TILE
    pair = jax.ShapeDtypeStruct((size, 2 * width), BF)
    if dq is None:
        dq_shape = jax.ShapeDtypeStruct((4, heads, TILE, size), F32)
    else:
        dq_shape = jax.ShapeDtypeStruct((4, size, width), BF)
    return pl.pallas_call(
        functools.partial(backward_kernel, scale2, factor, dq is None),
        out_shape=(pair, pair, dq_shape),
        scratch_shapes=[
            pltpu.VMEM((4, size, width), BF),
            pltpu.VMEM((4, size, width), BF),
            pltpu.VMEM((2 * size, width), BF),
            pltpu.VMEM((2 * size, width), BF),
            pltpu.VMEM((heads, TILE, 2 * size), BF),
            pltpu.VMEM((2 * size, width), F32),
            pltpu.VMEM((2 * size, width), F32),
        ],
        compiler_params=params(),
        name="backward",
    )(*queries, *grads, *pairs, lse, delta, bias, *([] if dq is None else [dq]))


def spread_kernel(place, dq, dkv, w_ref, o0, o1, o2, o3, rows):
    height = o0.shape[0] // 2
    width = dq.shape[1]

    @pl.when(pl.program_id(0) == 0)
    def _():
        for i in range(8):
            at = pl.ds(pl.multiple_of(place[i] * height, 16), height)
            to = slice(i * height, (i + 1) * height)
            rows[to, :width] = dq[at, :]
            rows[to, width:] = dkv[at, :]

    total = sum(dot_nt(rows[:, c * width : (c + 1) * width], w_ref[c]) for c in range(3)).astype(BF)
    for i, out in enumerate((o0, o1, o2, o3)):
        out[...] = total[2 * i * height : 2 * (i + 1) * height]


def spread(place, dq, dkv, weight, half, chunk=512):
    total, width = dq.shape
    columns = weight.shape[1] // 2
    steps = columns // chunk
    out = jax.ShapeDtypeStruct((total // 4, columns), BF)
    return pl.pallas_call(
        spread_kernel,
        out_shape=(out,) * 4,
        grid_spec=pltpu.PrefetchScalarGridSpec(
            num_scalar_prefetch=1,
            grid=(steps,),
            in_specs=[
                pl.BlockSpec((total, width), lambda k, place: (0, 0)),
                pl.BlockSpec((total, 2 * width), lambda k, place: (0, 0)),
                pl.BlockSpec((3, chunk, width), lambda k, place: (0, k + half * steps, 0)),
            ],
            out_specs=(pl.BlockSpec((total // 4, chunk), lambda k, place: (0, k)),) * 4,
            scratch_shapes=[pltpu.VMEM((total, 3 * width), BF)],
        ),
        compiler_params=params(),
        name="spread",
    )(place, dq, dkv, weight)


def body(hidden_states, qkv_weight, out_grad, tile_frame, frame_band):
    heads = frame_band.shape[0]
    width = qkv_weight.shape[2]
    head_dim = width // heads
    factor = 1.0 / math.sqrt(head_dim)
    scale2 = factor * math.log2(math.e)
    slabs, shards = lax.axis_size("slab"), lax.axis_size("head")
    slab, shard = lax.axis_index("slab"), lax.axis_index("head")
    height, model = hidden_states.shape
    half = model // 2
    slab_tiles = tile_frame.shape[0] // slabs

    def along_y(x, k):
        return lax.ppermute(x, "slab", [(i, (i + 4 * k) % slabs) for i in range(slabs)])

    def across_x(x):
        return lax.ppermute(x, "slab", [(i, i ^ 2) for i in range(slabs)])

    def across_core(x):
        return lax.ppermute(x, "slab", [(i, i ^ 1) for i in range(slabs)])

    def along_z(x, k):
        return lax.ppermute(x, "head", [(i, (i + 2 * k) % shards) for i in range(shards)])

    def across_far(x):
        return lax.ppermute(x, "head", [(i, i ^ 1) for i in range(shards)])

    z, far = shard // 2, shard % 2
    place = jnp.stack([((z + dz) % 4) * 2 + (far ^ dx) for dz in STEPS for dx in (0, 1)]).astype(jnp.int32)

    y, low = slab // 4, slab % 4
    frames = tile_frame.reshape(slabs, slab_tiles)
    query_frames = jnp.stack([frames[((y + d) % 4) * 4 + low] for d in STEPS])
    key_frames = jnp.concatenate([frames[y * 4 + (low ^ d)] for d in (0, 1, 2, 3)])
    distance = jnp.abs(query_frames[:, None, :] - key_frames[None, :, None])
    inside = distance[:, None] <= frame_band[None, :, None, None]
    bias = jnp.repeat(jnp.where(inside, 0.0, -FAR).astype(F32), TILE, axis=3)

    a, b = hidden_states[:, :half], hidden_states[:, half:]
    fa, fb = across_far(a), across_far(b)
    up = [along_z(x, 1) for x in (a, b, fa, fb)]
    down = [along_z(x, -1) for x in (a, b, fa, fb)]
    two_a = [along_z(up[0], 1), along_z(up[2], 1)]
    two_b = [along_z(down[1], -1), along_z(down[3], -1)]
    first = [a, fa, up[0], up[2], down[0], down[2], two_a[0], two_a[1]]
    second = [b, fb, up[1], up[3], down[1], down[3], two_b[0], two_b[1]]
    grads = [out_grad, along_y(out_grad, 1), along_y(out_grad, -1), along_y(out_grad, 2)]

    acc = project(place, first, qkv_weight, 0)
    queries_own, pair_own = project(place, second, qkv_weight, 1, acc)

    queries = [queries_own, along_y(queries_own, 1), along_y(queries_own, -1), along_y(queries_own, 2)]
    pair_x = across_x(pair_own)
    pairs = [pair_own, across_core(pair_own), pair_x, across_core(pair_x)]

    out_t, stat = forward(scale2, queries, grads, pairs, bias)
    stats = [stat, along_y(stat, 1), along_y(stat, -1), along_y(stat, 2)]
    lse, delta = totals(stats)

    def home(blocks):
        return [blocks[0], along_y(blocks[2], 1), along_y(blocks[1], -1), along_y(blocks[3], 2)]

    tiles = 2 * slab_tiles
    dx, dxc, dq = backward(
        scale2, factor, queries, grads, pairs[2:], lse, delta, bias[:, :, tiles:]
    )
    near = across_x(dx + across_core(dxc))
    down_own, down_core, dq = backward(
        scale2, factor, queries, grads, pairs[:2], lse, delta, bias[:, :, :tiles], dq
    )
    attn_out = merge(home(out_t), stats)
    pair_grad = (
        down_own.astype(F32) + across_core(down_core).astype(F32) + near.astype(F32)
    ).astype(BF)
    query_grad = sum(x.astype(F32) for x in home(dq)).astype(BF)

    done = []
    for which in (0, 1):
        own, prev, succ, two = spread(place, query_grad, pair_grad, qkv_weight, which)
        if which == 0:
            succ = succ + along_z(two, 1)
        else:
            prev = prev + along_z(two, -1)
        got = own.astype(F32) + along_z(succ, 1).astype(F32) + along_z(prev, -1).astype(F32)
        other = across_far(got[height:].astype(BF))
        done.append((got[:height] + other.astype(F32)).astype(BF))
    return (attn_out, jnp.concatenate(done, axis=1))


def solution(mesh):
    placed = (P(("slab", "head"), None), P(None, None, "head"), P("slab", "head"), P(), P("head"))
    return jax.shard_map(
        body,
        mesh=mesh,
        in_specs=placed,
        out_specs=(P("slab", "head"), P(("slab", "head"), None)),
        check_vma=False,
    )
```

```python
import functools
import math

import jax
import jax.numpy as jnp
from jax import lax
from jax.experimental import pallas as pl
from jax.experimental.pallas import tpu as pltpu
from jax.sharding import PartitionSpec as P

TILE = 128
BF = jnp.bfloat16
F32 = jnp.float32
NT_DIMS = (((1,), (1,)), ((), ()))
FAR = 1e30
FROM = ((0, 1, 2, 3), (2, 0, 3, 1), (1, 3, 0, 2), (3, 2, 1, 0))
STEPS = (0, -1, 1, 2)


def params(mebibytes):
    return pltpu.CompilerParams(vmem_limit_bytes=mebibytes * 1024 * 1024)


def after(x, *others):
    return lax.optimization_barrier((x, others))[0]


def cost(micros):
    return pl.CostEstimate(flops=int(micros * 1.15e9), bytes_accessed=0, transcendentals=0)


def dot(a, b):
    return jnp.dot(a, b, preferred_element_type=F32)


def dot_nt(a, b):
    return lax.dot_general(a, b, NT_DIMS, preferred_element_type=F32)


def project_kernel(count, height, first, last, place, *refs):
    blocks, w_ref = refs[:count], refs[count]
    acc_in = None if first else refs[count + 1]
    outs, (rows, acc) = refs[count + (1 if first else 2) : -2], refs[-2:]
    step = pl.program_id(0)

    @pl.when(step == 0)
    def _():
        if first:
            acc[...] = jnp.zeros_like(acc)
        else:
            acc[...] = acc_in[...]

    i = 0
    for block in blocks:
        for r in range(0, block.shape[0], height):
            rows[pl.ds(pl.multiple_of(place[i] * height, 16), height), :] = block[r : r + height, :]
            i += 1
    side = dot(rows[...], jnp.concatenate([w_ref[c] for c in range(3)], axis=1))
    width = w_ref.shape[2]
    for c in range(3):
        acc[c] += side[:, c * width : (c + 1) * width]

    @pl.when(step == pl.num_programs(0) - 1)
    def _():
        if last:
            q_ref, kv_ref = outs
            q_ref[...] = acc[0].astype(BF)
            kv_ref[:, :width] = acc[1].astype(BF)
            kv_ref[:, width:] = acc[2].astype(BF)
        else:
            outs[0][...] = acc[...]


def project(place, blocks, weight, start, acc=None, last=False, chunk=1024):
    columns, width = blocks[0].shape[1], weight.shape[2]
    total = sum(b.shape[0] for b in blocks)
    height = total // place.shape[0]
    skip = start // chunk
    whole = pl.BlockSpec((3, total, width), lambda k, place: (0, 0, 0))
    if last:
        out_shape = (
            jax.ShapeDtypeStruct((total, width), BF),
            jax.ShapeDtypeStruct((total, 2 * width), BF),
        )
        out_specs = (
            pl.BlockSpec((total, width), lambda k, place: (0, 0)),
            pl.BlockSpec((total, 2 * width), lambda k, place: (0, 0)),
        )
    else:
        out_shape, out_specs = jax.ShapeDtypeStruct((3, total, width), F32), whole
    return pl.pallas_call(
        functools.partial(project_kernel, len(blocks), height, acc is None, last),
        out_shape=out_shape,
        grid_spec=pltpu.PrefetchScalarGridSpec(
            num_scalar_prefetch=1,
            grid=(columns // chunk,),
            in_specs=[pl.BlockSpec((b.shape[0], chunk), lambda k, place: (0, k)) for b in blocks]
            + [pl.BlockSpec((3, chunk, width), lambda k, place: (0, k + skip, 0))]
            + ([] if acc is None else [whole]),
            out_specs=out_specs,
            scratch_shapes=[pltpu.VMEM((total, chunk), BF), pltpu.VMEM((3, total, width), F32)],
        ),
        compiler_params=params(18),
        cost_estimate=cost(6),
        name="project",
    )(place, *blocks, weight, *([] if acc is None else [acc]))


def forward_kernel(scale2, q0, q1, q2, q3, g0, g1, g2, g3, kv0, kv1, kv2, kv3, bias, ot, stat, qs, gt, kv, vt):
    size, width = q0.shape
    heads = width // TILE
    for b, (q, g, k) in enumerate(((q0, g0, kv0), (q1, g1, kv1), (q2, g2, kv2), (q3, g3, kv3))):
        qs[b] = q[...]
        kv[b * size : (b + 1) * size, :] = k[:, :width]
        for h in range(heads):
            at = slice(h * TILE, (h + 1) * TILE)
            gt[b, h] = g[:, at].T
            vt[h, :, b * size : (b + 1) * size] = k[:, width + h * TILE : width + (h + 1) * TILE].T
    tiles = kv.shape[0] // TILE

    def step(b, carry):
        for h in range(heads):
            at = slice(h * TILE, (h + 1) * TILE)
            s = dot_nt(kv[:, at], qs[b, :, at])
            away = bias[b, h]
            peak = jnp.full((1, size), -FAR, F32)
            for t in range(tiles):
                top = jnp.max(s[t * TILE : (t + 1) * TILE], axis=0, keepdims=True) * scale2
                peak = jnp.maximum(peak, top + away[t : t + 1])
            total = jnp.zeros((1, size), F32)
            parts = []
            for t in range(tiles):
                base = jnp.where(away[t : t + 1] < 0, FAR, peak)
                p = jnp.exp2(s[t * TILE : (t + 1) * TILE] * scale2 - base)
                total = total + jnp.sum(p, axis=0, keepdims=True)
                parts.append(p.astype(BF))
            o = dot(vt[h], jnp.concatenate(parts, axis=0))
            stat[b, 3 * h : 3 * h + 1, :] = peak
            stat[b, 3 * h + 1 : 3 * h + 2, :] = total
            stat[b, 3 * h + 2 : 3 * h + 3, :] = jnp.sum(o * gt[b, h].astype(F32), axis=0, keepdims=True)
            ot[b, h] = (o * jnp.where(total > 0, 1.0 / total, 0.0)).astype(BF)
        return carry

    lax.fori_loop(0, 4, step, 0)


def forward(scale2, queries, grads, pairs, bias):
    size, width = queries[0].shape
    heads = width // TILE
    return pl.pallas_call(
        functools.partial(forward_kernel, scale2),
        out_shape=(
            jax.ShapeDtypeStruct((4, heads, TILE, size), BF),
            jax.ShapeDtypeStruct((4, 3 * heads, size), F32),
        ),
        scratch_shapes=[
            pltpu.VMEM((4, size, width), BF),
            pltpu.VMEM((4, heads, TILE, size), BF),
            pltpu.VMEM((4 * size, width), BF),
            pltpu.VMEM((heads, TILE, 4 * size), BF),
        ],
        compiler_params=params(24),
        cost_estimate=cost(17), name="forward",
    )(*queries, *grads, *pairs, bias)


def totals_kernel(s0, s1, s2, s3, lse_ref, delta_ref):
    heads = lse_ref.shape[1]
    sources = (s0, s1, s2, s3)
    for p in range(4):
        for h in range(heads):
            rows = [
                [s[FROM[j][p], 3 * h + i : 3 * h + i + 1, :] for i in range(3)]
                for j, s in enumerate(sources)
            ]
            peak = functools.reduce(jnp.maximum, [r[0] for r in rows])
            shrink = [jnp.exp2(r[0] - peak) for r in rows]
            total = sum(r[1] * f for r, f in zip(rows, shrink))
            lse_ref[p, h : h + 1, :] = peak + jnp.log2(total)
            delta_ref[p, h : h + 1, :] = sum(r[2] * f for r, f in zip(rows, shrink)) / total


def totals(stats):
    _, rows, size = stats[0].shape
    shape = jax.ShapeDtypeStruct((4, rows // 3, size), F32)
    return pl.pallas_call(totals_kernel, out_shape=(shape, shape), compiler_params=params(6), cost_estimate=cost(2), name="totals")(*stats)


def merge_kernel(o0, o1, o2, o3, s0, s1, s2, s3, out):
    heads = o0.shape[0]
    for h in range(heads):
        rows = [
            [s[FROM[j][0], 3 * h + i : 3 * h + i + 1, :] for i in range(2)]
            for j, s in enumerate((s0, s1, s2, s3))
        ]
        peak = functools.reduce(jnp.maximum, [r[0] for r in rows])
        shares = [r[1] * jnp.exp2(r[0] - peak) for r in rows]
        whole = sum(shares)
        o = sum(x[h].astype(F32) * (share / whole) for x, share in zip((o0, o1, o2, o3), shares))
        out[:, h * TILE : (h + 1) * TILE] = o.T.astype(BF)


def merge(outs, stats):
    heads, _, size = outs[0].shape
    return pl.pallas_call(
        merge_kernel,
        out_shape=jax.ShapeDtypeStruct((size, heads * TILE), BF),
        compiler_params=params(6),
        cost_estimate=cost(2), name="merge",
    )(*outs, *stats)


def backward_kernel(scale2, factor, count, chained, last, places, *refs):
    q_refs, refs = refs[:count], refs[count:]
    g_refs, refs = refs[:count], refs[count:]
    (kv_a, kv_b, lse, delta, bias), refs = refs[:5], refs[5:]
    if chained:
        (dq_in, dk_in, dv_in), refs = refs[:3], refs[3:]
    else:
        dq_in = dk_in = dv_in = None
    outs, (qs, gs, ks, vs, kt, dk, dv) = refs[:-7], refs[-7:]
    finish = dq_in is not None
    dq_out = outs[0]
    size, width = q_refs[0].shape
    heads = width // TILE
    for b in range(count):
        qs[b] = q_refs[b][...]
        gs[b] = g_refs[b][...]
    for i, k in enumerate((kv_a, kv_b)):
        ks[i * size : (i + 1) * size, :] = k[:, :width]
        vs[i * size : (i + 1) * size, :] = k[:, width:]
        for h in range(heads):
            kt[h, :, i * size : (i + 1) * size] = k[:, h * TILE : (h + 1) * TILE].T
    if dk_in is None:
        dk[...] = jnp.zeros_like(dk)
        dv[...] = jnp.zeros_like(dv)
    else:
        dk[...] = dk_in[...]
        dv[...] = dv_in[...]
    tiles = 2 * size // TILE

    def step(b, carry):
        p0 = places + b
        for h in range(heads):
            at = slice(h * TILE, (h + 1) * TILE)
            q, g = qs[b, :, at], gs[b, :, at]
            s = dot_nt(ks[:, at], q)
            dp = dot_nt(vs[:, at], g)
            away, top, shift = bias[p0, h], lse[p0, h : h + 1], delta[p0, h : h + 1]
            probs, grads = [], []
            for t in range(tiles):
                rows = slice(t * TILE, (t + 1) * TILE)
                base = jnp.where(away[t : t + 1] < 0, FAR, top)
                p = jnp.exp2(s[rows] * scale2 - base)
                probs.append(p.astype(BF))
                grads.append((p * (dp[rows] - shift)).astype(BF))
            p = jnp.concatenate(probs, axis=0)
            ds = jnp.concatenate(grads, axis=0)
            dv[:, at] += dot(p, g)
            dk[:, at] += dot(ds, q)
            dq = dot(kt[h], ds)
            if finish:
                dq_out[b, :, at] = ((dq_in[p0, h] + dq) * factor).T.astype(BF)
            else:
                dq_out[b, h] = dq
        return carry

    lax.fori_loop(0, count, step, 0)
    if last:
        for i, out in enumerate(outs[1:]):
            rows = slice(i * size, (i + 1) * size)
            out[:, :width] = (dk[rows] * factor).astype(BF)
            out[:, width:] = dv[rows].astype(BF)
    else:
        outs[1][...] = dk[...]
        outs[2][...] = dv[...]


def backward(scale2, factor, queries, grads, pairs, lse, delta, bias, places=0, dq=None, sums=None, last=True):
    size, width = queries[0].shape
    heads, count = width // TILE, len(queries)
    if last:
        tail = (jax.ShapeDtypeStruct((size, 2 * width), BF),) * 2
    else:
        tail = (jax.ShapeDtypeStruct((2 * size, width), F32),) * 2
    if dq is None:
        head = jax.ShapeDtypeStruct((count, heads, TILE, size), F32)
    else:
        head = jax.ShapeDtypeStruct((count, size, width), BF)
    chained = dq is not None
    extra = [dq, *sums] if sums is not None else ([dq] if chained else [])

    def kernel(*refs):
        refs = list(refs)
        if chained and sums is None:
            at = 2 * count + 6
            refs[at:at] = [None, None]
        backward_kernel(scale2, factor, count, chained, last, places, *refs)

    return pl.pallas_call(
        kernel,
        out_shape=(head, *tail),
        scratch_shapes=[
            pltpu.VMEM((count, size, width), BF),
            pltpu.VMEM((count, size, width), BF),
            pltpu.VMEM((2 * size, width), BF),
            pltpu.VMEM((2 * size, width), BF),
            pltpu.VMEM((heads, TILE, 2 * size), BF),
            pltpu.VMEM((2 * size, width), F32),
            pltpu.VMEM((2 * size, width), F32),
        ],
        compiler_params=params(26),
        cost_estimate=cost(4 * count), name="backward",
    )(*queries, *grads, *pairs, lse, delta, bias, *extra)


def spread_kernel(height, place, dq, dkv, w_ref, *refs):
    outs, rows = refs[:-1], refs[-1]
    width = dq.shape[1]

    @pl.when(pl.program_id(0) == 0)
    def _():
        for i in range(place.shape[0]):
            at = pl.ds(pl.multiple_of(place[i] * height, 16), height)
            to = slice(i * height, (i + 1) * height)
            rows[to, :width] = dq[at, :]
            rows[to, width:] = dkv[at, :]

    total = sum(dot_nt(rows[:, c * width : (c + 1) * width], w_ref[c]) for c in range(3)).astype(BF)
    at = 0
    for out in outs:
        out[...] = total[at : at + out.shape[0]]
        at += out.shape[0]


def spread(place, dq, dkv, weight, start, columns, sizes, chunk=1024):
    total, width = dq.shape
    height = total // place.shape[0]
    skip = start // chunk
    return pl.pallas_call(
        functools.partial(spread_kernel, height),
        out_shape=tuple(jax.ShapeDtypeStruct((n * height, columns), BF) for n in sizes),
        grid_spec=pltpu.PrefetchScalarGridSpec(
            num_scalar_prefetch=1,
            grid=(columns // chunk,),
            in_specs=[
                pl.BlockSpec((total, width), lambda k, place: (0, 0)),
                pl.BlockSpec((total, 2 * width), lambda k, place: (0, 0)),
                pl.BlockSpec((3, chunk, width), lambda k, place: (0, k + skip, 0)),
            ],
            out_specs=tuple(pl.BlockSpec((n * height, chunk), lambda k, place: (0, k)) for n in sizes),
            scratch_shapes=[pltpu.VMEM((total, 3 * width), BF)],
        ),
        compiler_params=params(20),
        cost_estimate=cost(0.3),
        name="spread",
    )(place, dq, dkv, weight)


def body(hidden_states, qkv_weight, out_grad, tile_frame, frame_band):
    heads = frame_band.shape[0]
    width = qkv_weight.shape[2]
    head_dim = width // heads
    factor = 1.0 / math.sqrt(head_dim)
    scale2 = factor * math.log2(math.e)
    slabs, shards = lax.axis_size("slab"), lax.axis_size("head")
    slab, shard = lax.axis_index("slab"), lax.axis_index("head")
    height, model = hidden_states.shape
    part = model // 3
    slab_tiles = tile_frame.shape[0] // slabs

    def along_y(x, k):
        return lax.ppermute(x, "slab", [(i, (i + 4 * k) % slabs) for i in range(slabs)])

    def across_x(x):
        return lax.ppermute(x, "slab", [(i, i ^ 2) for i in range(slabs)])

    def across_core(x):
        return lax.ppermute(x, "slab", [(i, i ^ 1) for i in range(slabs)])

    def along_z(x, k):
        return lax.ppermute(x, "head", [(i, (i + 2 * k) % shards) for i in range(shards)])

    def across_far(x):
        return lax.ppermute(x, "head", [(i, i ^ 1) for i in range(shards)])

    z, far = shard // 2, shard % 2
    def places(shifts):
        return jnp.stack([((z + dz) % 4) * 2 + (far ^ dx) for dz, dx in shifts]).astype(jnp.int32)

    by_z = places([(dz, dx) for dz in STEPS for dx in (0, 1)])
    by_x = places([(dz, dx) for dx in (0, 1) for dz in STEPS])

    y, low = slab // 4, slab % 4
    frames = tile_frame.reshape(slabs, slab_tiles)
    query_frames = jnp.stack([frames[((y + d) % 4) * 4 + low] for d in STEPS])
    key_frames = jnp.concatenate([frames[y * 4 + (low ^ d)] for d in (0, 1, 2, 3)])
    distance = jnp.abs(query_frames[:, None, :] - key_frames[None, :, None])
    inside = distance[:, None] <= frame_band[None, :, None, None]
    bias = jnp.repeat(jnp.where(inside, 0.0, -FAR).astype(F32), TILE, axis=3)

    c, a, b = (hidden_states[:, i * part : (i + 1) * part] for i in range(3))
    up_c, down_c, two_c = along_z(c, 1), along_z(c, -1), along_z(c, 2)
    far_a = across_far(a)
    all_c = jnp.concatenate([c, up_c, down_c, two_c])
    far_c = across_far(all_c)
    pair_a = jnp.concatenate([a, far_a])
    up_a, down_a = along_z(pair_a, 1), along_z(pair_a, -1)
    b = after(b, far_a)
    pair_b = jnp.concatenate([b, across_far(b)])
    up_b, down_b = along_z(pair_b, 1), along_z(pair_b, -1)
    two_a, two_b = along_z(up_a, 1), along_z(down_b, -1)
    grads = [out_grad, along_y(out_grad, 1)]
    grads.append(along_y(after(out_grad, grads[1]), -1))
    grads.append(along_y(after(out_grad, grads[2]), 2))

    streamed = pltpu.with_memory_space_constraint(qkv_weight, pltpu.HBM)
    acc = project(by_z, [pair_a, up_a, down_a, two_a], streamed, part)
    acc = project(by_x, [all_c, far_c], qkv_weight, 0, acc)
    acc, bias, grads[1:] = lax.optimization_barrier((acc, bias, grads[1:]))
    queries_own, pair_own = project(
        by_z, [pair_b, up_b, down_b, two_b], qkv_weight, 2 * part, acc, True
    )

    pair_x = across_x(pair_own)
    queries = [queries_own, along_y(queries_own, 1), along_y(queries_own, -1), along_y(queries_own, 2)]
    pair_x, queries[1:] = after((pair_x, queries[1:]), pair_own)
    pairs = [pair_own, across_core(pair_own), pair_x, across_core(pair_x)]

    out_t, stat = forward(scale2, queries, grads, pairs, bias)
    stats = [stat, along_y(stat, 1), along_y(stat, -1), along_y(stat, 2)]
    lse, delta = totals(stats)

    tiles = 2 * slab_tiles
    back = functools.partial(backward, scale2, factor)
    out_t = after(out_t, lse)
    outs = [out_t[0], along_y(out_t[2], 1), along_y(out_t[1], -1), along_y(out_t[3], 2)]
    dq, dx, dxc = back(queries, grads, pairs[2:], lse, delta, bias[:, :, tiles:])
    dq, dx, dxc, outs = lax.optimization_barrier((dq, dx, dxc, outs))
    dq, near = after((dq, dx + across_core(dxc)), dq)
    near = across_x(near)
    close = bias[:, :, :tiles]
    dqs, *sums = back(queries[1:], grads[1:], pairs[:2], lse, delta, close, 1, dq, None, False)
    got = [along_y(dqs[1], 1), along_y(dqs[0], -1), along_y(dqs[2], 2)]
    attn_out = merge(outs, stats)
    dq, near, attn_out = after((dq, near, attn_out), dqs)
    dq0, down_own, down_core = back(queries[:1], grads[:1], pairs[:2], lse, delta, close, 0, dq, sums)
    down_core, got = after((down_core, got), dq0)
    pair_grad = (
        down_own.astype(F32) + across_core(down_core).astype(F32) + near.astype(F32)
    ).astype(BF)
    query_grad = sum(x.astype(F32) for x in (dq0[0], *got)).astype(BF)

    send = functools.partial(spread, dkv=pair_grad, weight=qkv_weight, columns=part)
    own_a, prev_a, succ_a, out_a = send(by_z, query_grad, start=part, sizes=(2, 2, 2, 2))
    got_a, from_a = along_z(out_a, 1), along_z(prev_a, -1)
    own_c, prev_c, succ_c, out_c, other_c = send(
        by_x, after(query_grad, own_a), start=0, sizes=(1, 1, 1, 1, 4)
    )
    came_c = across_far(other_c)
    own_b, prev_b, succ_b, out_b = send(
        by_z, after(query_grad, own_c), start=2 * part, sizes=(2, 2, 2, 2)
    )
    out_b = after(out_b, from_a)
    got_b, from_b = along_z(out_b, -1), along_z(succ_b, 1)
    back_a = along_z(succ_a + got_a, 1)
    back_b = along_z(prev_b + got_b, -1)
    own_c, prev_c, succ_c, out_c = (
        (x.astype(F32) + came_c[i * height : (i + 1) * height].astype(F32)).astype(BF)
        for i, x in enumerate((own_c, prev_c, succ_c, out_c))
    )
    sums_c = (own_c, along_z(succ_c, 1), along_z(prev_c, -1), along_z(out_c, 2))
    done = [sum(x.astype(F32) for x in sums_c).astype(BF)]
    for own, one, other in ((own_a, from_a, back_a), (own_b, from_b, back_b)):
        total = own.astype(F32) + one.astype(F32) + other.astype(F32)
        rest = across_far(total[height:].astype(BF))
        done.append((total[:height] + rest.astype(F32)).astype(BF))
    return (attn_out, jnp.concatenate(done, axis=1))


def solution(mesh):
    placed = (P(("slab", "head"), None), P(None, None, "head"), P("slab", "head"), P(), P("head"))
    return jax.shard_map(
        body,
        mesh=mesh,
        in_specs=placed,
        out_specs=(P("slab", "head"), P(("slab", "head"), None)),
        check_vma=False,
    )
```

```python
import functools
import math

import jax
import jax.numpy as jnp
from jax import lax
from jax.experimental import pallas as pl
from jax.experimental.pallas import tpu as pltpu
from jax.sharding import PartitionSpec as P

TILE = 128
BF = jnp.bfloat16
F32 = jnp.float32
NT_DIMS = (((1,), (1,)), ((), ()))
FAR = 1e30
FROM = ((0, 1, 2, 3), (2, 0, 3, 1), (1, 3, 0, 2), (3, 2, 1, 0))
STEPS = (0, -1, 1, 2)


def params(mebibytes):
    return pltpu.CompilerParams(vmem_limit_bytes=mebibytes * 1024 * 1024)


def after(x, *others):
    return lax.optimization_barrier((x, others))[0]


def cost(micros):
    return pl.CostEstimate(flops=int(micros * 1.15e9), bytes_accessed=0, transcendentals=0)


def dot(a, b):
    return jnp.dot(a, b, preferred_element_type=F32)


def dot_nt(a, b):
    return lax.dot_general(a, b, NT_DIMS, preferred_element_type=F32)


def project_kernel(count, height, first, last, place, *refs):
    blocks, w_ref = refs[:count], refs[count]
    acc_in = None if first else refs[count + 1]
    outs, (rows, acc) = refs[count + (1 if first else 2) : -2], refs[-2:]
    step = pl.program_id(0)

    @pl.when(step == 0)
    def _():
        if first:
            acc[...] = jnp.zeros_like(acc)
        else:
            acc[...] = acc_in[...]

    i = 0
    for block in blocks:
        for r in range(0, block.shape[0], height):
            rows[pl.ds(pl.multiple_of(place[i] * height, 16), height), :] = block[r : r + height, :]
            i += 1
    side = dot(rows[...], jnp.concatenate([w_ref[c] for c in range(3)], axis=1))
    width = w_ref.shape[2]
    for c in range(3):
        acc[c] += side[:, c * width : (c + 1) * width]

    @pl.when(step == pl.num_programs(0) - 1)
    def _():
        if last:
            q_ref, kv_ref = outs
            q_ref[...] = acc[0].astype(BF)
            kv_ref[:, :width] = acc[1].astype(BF)
            kv_ref[:, width:] = acc[2].astype(BF)
        else:
            outs[0][...] = acc[...]


def project(place, blocks, weight, start, acc=None, last=False, chunk=1024):
    columns, width = blocks[0].shape[1], weight.shape[2]
    total = sum(b.shape[0] for b in blocks)
    height = total // place.shape[0]
    skip = start // chunk
    whole = pl.BlockSpec((3, total, width), lambda k, place: (0, 0, 0))
    if last:
        out_shape = (
            jax.ShapeDtypeStruct((total, width), BF),
            jax.ShapeDtypeStruct((total, 2 * width), BF),
        )
        out_specs = (
            pl.BlockSpec((total, width), lambda k, place: (0, 0)),
            pl.BlockSpec((total, 2 * width), lambda k, place: (0, 0)),
        )
    else:
        out_shape, out_specs = jax.ShapeDtypeStruct((3, total, width), F32), whole
    return pl.pallas_call(
        functools.partial(project_kernel, len(blocks), height, acc is None, last),
        out_shape=out_shape,
        grid_spec=pltpu.PrefetchScalarGridSpec(
            num_scalar_prefetch=1,
            grid=(columns // chunk,),
            in_specs=[pl.BlockSpec((b.shape[0], chunk), lambda k, place: (0, k)) for b in blocks]
            + [pl.BlockSpec((3, chunk, width), lambda k, place: (0, k + skip, 0))]
            + ([] if acc is None else [whole]),
            out_specs=out_specs,
            scratch_shapes=[pltpu.VMEM((total, chunk), BF), pltpu.VMEM((3, total, width), F32)],
        ),
        compiler_params=params(18),
        cost_estimate=cost(6),
        name="project",
    )(place, *blocks, weight, *([] if acc is None else [acc]))


def forward_kernel(scale2, q0, q1, q2, q3, g0, g1, g2, g3, kv0, kv1, kv2, kv3, bias, ot, stat, qs, gt, kv, vt):
    size, width = q0.shape
    heads = width // TILE
    for b, (q, g, k) in enumerate(((q0, g0, kv0), (q1, g1, kv1), (q2, g2, kv2), (q3, g3, kv3))):
        qs[b] = q[...]
        kv[b * size : (b + 1) * size, :] = k[:, :width]
        for h in range(heads):
            at = slice(h * TILE, (h + 1) * TILE)
            gt[b, h] = g[:, at].T
            vt[h, :, b * size : (b + 1) * size] = k[:, width + h * TILE : width + (h + 1) * TILE].T
    tiles = kv.shape[0] // TILE

    def step(b, carry):
        for h in range(heads):
            at = slice(h * TILE, (h + 1) * TILE)
            s = dot_nt(kv[:, at], qs[b, :, at])
            away = bias[b, h]
            peak = jnp.full((1, size), -FAR, F32)
            for t in range(tiles):
                top = jnp.max(s[t * TILE : (t + 1) * TILE], axis=0, keepdims=True) * scale2
                peak = jnp.maximum(peak, top + away[t : t + 1])
            total = jnp.zeros((1, size), F32)
            parts = []
            for t in range(tiles):
                base = jnp.where(away[t : t + 1] < 0, FAR, peak)
                p = jnp.exp2(s[t * TILE : (t + 1) * TILE] * scale2 - base)
                total = total + jnp.sum(p, axis=0, keepdims=True)
                parts.append(p.astype(BF))
            o = dot(vt[h], jnp.concatenate(parts, axis=0))
            stat[b, 3 * h : 3 * h + 1, :] = peak
            stat[b, 3 * h + 1 : 3 * h + 2, :] = total
            stat[b, 3 * h + 2 : 3 * h + 3, :] = jnp.sum(o * gt[b, h].astype(F32), axis=0, keepdims=True)
            ot[b, h] = (o * jnp.where(total > 0, 1.0 / total, 0.0)).astype(BF)
        return carry

    lax.fori_loop(0, 4, step, 0)


def forward(scale2, queries, grads, pairs, bias):
    size, width = queries[0].shape
    heads = width // TILE
    return pl.pallas_call(
        functools.partial(forward_kernel, scale2),
        out_shape=(
            jax.ShapeDtypeStruct((4, heads, TILE, size), BF),
            jax.ShapeDtypeStruct((4, 3 * heads, size), F32),
        ),
        scratch_shapes=[
            pltpu.VMEM((4, size, width), BF),
            pltpu.VMEM((4, heads, TILE, size), BF),
            pltpu.VMEM((4 * size, width), BF),
            pltpu.VMEM((heads, TILE, 4 * size), BF),
        ],
        compiler_params=params(24),
        cost_estimate=cost(17), name="forward",
    )(*queries, *grads, *pairs, bias)


def totals_kernel(s0, s1, s2, s3, lse_ref, delta_ref):
    heads = lse_ref.shape[1]
    sources = (s0, s1, s2, s3)
    for p in range(4):
        for h in range(heads):
            rows = [
                [s[FROM[j][p], 3 * h + i : 3 * h + i + 1, :] for i in range(3)]
                for j, s in enumerate(sources)
            ]
            peak = functools.reduce(jnp.maximum, [r[0] for r in rows])
            shrink = [jnp.exp2(r[0] - peak) for r in rows]
            total = sum(r[1] * f for r, f in zip(rows, shrink))
            lse_ref[p, h : h + 1, :] = peak + jnp.log2(total)
            delta_ref[p, h : h + 1, :] = sum(r[2] * f for r, f in zip(rows, shrink)) / total


def totals(stats):
    _, rows, size = stats[0].shape
    shape = jax.ShapeDtypeStruct((4, rows // 3, size), F32)
    return pl.pallas_call(totals_kernel, out_shape=(shape, shape), compiler_params=params(6), cost_estimate=cost(2), name="totals")(*stats)


def merge_kernel(o0, o1, o2, o3, s0, s1, s2, s3, out):
    heads = o0.shape[0]
    for h in range(heads):
        rows = [
            [s[FROM[j][0], 3 * h + i : 3 * h + i + 1, :] for i in range(2)]
            for j, s in enumerate((s0, s1, s2, s3))
        ]
        peak = functools.reduce(jnp.maximum, [r[0] for r in rows])
        shares = [r[1] * jnp.exp2(r[0] - peak) for r in rows]
        whole = sum(shares)
        o = sum(x[h].astype(F32) * (share / whole) for x, share in zip((o0, o1, o2, o3), shares))
        out[:, h * TILE : (h + 1) * TILE] = o.T.astype(BF)


def merge(outs, stats):
    heads, _, size = outs[0].shape
    return pl.pallas_call(
        merge_kernel,
        out_shape=jax.ShapeDtypeStruct((size, heads * TILE), BF),
        compiler_params=params(6),
        cost_estimate=cost(2), name="merge",
    )(*outs, *stats)


def backward_kernel(scale2, factor, count, chained, last, places, *refs):
    q_refs, refs = refs[:count], refs[count:]
    g_refs, refs = refs[:count], refs[count:]
    (kv_a, kv_b, lse, delta, bias), refs = refs[:5], refs[5:]
    if chained:
        (dq_in, dk_in, dv_in), refs = refs[:3], refs[3:]
    else:
        dq_in = dk_in = dv_in = None
    outs, (qs, gs, ks, vs, kt, dk, dv) = refs[:-7], refs[-7:]
    finish = dq_in is not None
    dq_out = outs[0]
    size, width = q_refs[0].shape
    heads = width // TILE
    for b in range(count):
        qs[b] = q_refs[b][...]
        gs[b] = g_refs[b][...]
    for i, k in enumerate((kv_a, kv_b)):
        ks[i * size : (i + 1) * size, :] = k[:, :width]
        vs[i * size : (i + 1) * size, :] = k[:, width:]
        for h in range(heads):
            kt[h, :, i * size : (i + 1) * size] = k[:, h * TILE : (h + 1) * TILE].T
    if dk_in is None:
        dk[...] = jnp.zeros_like(dk)
        dv[...] = jnp.zeros_like(dv)
    else:
        dk[...] = dk_in[...]
        dv[...] = dv_in[...]
    tiles = 2 * size // TILE

    def step(b, carry):
        p0 = places + b
        for h in range(heads):
            at = slice(h * TILE, (h + 1) * TILE)
            q, g = qs[b, :, at], gs[b, :, at]
            s = dot_nt(ks[:, at], q)
            dp = dot_nt(vs[:, at], g)
            away, top, shift = bias[p0, h], lse[p0, h : h + 1], delta[p0, h : h + 1]
            probs, grads = [], []
            for t in range(tiles):
                rows = slice(t * TILE, (t + 1) * TILE)
                base = jnp.where(away[t : t + 1] < 0, FAR, top)
                p = jnp.exp2(s[rows] * scale2 - base)
                probs.append(p.astype(BF))
                grads.append((p * (dp[rows] - shift)).astype(BF))
            p = jnp.concatenate(probs, axis=0)
            ds = jnp.concatenate(grads, axis=0)
            dv[:, at] += dot(p, g)
            dk[:, at] += dot(ds, q)
            dq = dot(kt[h], ds)
            if finish:
                dq_out[b, :, at] = ((dq_in[p0, h] + dq) * factor).T.astype(BF)
            else:
                dq_out[b, h] = dq
        return carry

    lax.fori_loop(0, count, step, 0)
    if last:
        for i, out in enumerate(outs[1:]):
            rows = slice(i * size, (i + 1) * size)
            out[:, :width] = (dk[rows] * factor).astype(BF)
            out[:, width:] = dv[rows].astype(BF)
    else:
        outs[1][...] = dk[...]
        outs[2][...] = dv[...]


def backward(scale2, factor, queries, grads, pairs, lse, delta, bias, places=0, dq=None, sums=None, last=True):
    size, width = queries[0].shape
    heads, count = width // TILE, len(queries)
    if last:
        tail = (jax.ShapeDtypeStruct((size, 2 * width), BF),) * 2
    else:
        tail = (jax.ShapeDtypeStruct((2 * size, width), F32),) * 2
    if dq is None:
        head = jax.ShapeDtypeStruct((count, heads, TILE, size), F32)
    else:
        head = jax.ShapeDtypeStruct((count, size, width), BF)
    chained = dq is not None
    extra = [dq, *sums] if sums is not None else ([dq] if chained else [])

    def kernel(*refs):
        refs = list(refs)
        if chained and sums is None:
            at = 2 * count + 6
            refs[at:at] = [None, None]
        backward_kernel(scale2, factor, count, chained, last, places, *refs)

    return pl.pallas_call(
        kernel,
        out_shape=(head, *tail),
        scratch_shapes=[
            pltpu.VMEM((count, size, width), BF),
            pltpu.VMEM((count, size, width), BF),
            pltpu.VMEM((2 * size, width), BF),
            pltpu.VMEM((2 * size, width), BF),
            pltpu.VMEM((heads, TILE, 2 * size), BF),
            pltpu.VMEM((2 * size, width), F32),
            pltpu.VMEM((2 * size, width), F32),
        ],
        compiler_params=params(26),
        cost_estimate=cost(4 * count), name="backward",
    )(*queries, *grads, *pairs, lse, delta, bias, *extra)


def spread_kernel(height, place, dq, dkv, w_ref, *refs):
    outs, rows = refs[:-1], refs[-1]
    width = dq.shape[1]

    @pl.when(pl.program_id(0) == 0)
    def _():
        for i in range(place.shape[0]):
            at = pl.ds(pl.multiple_of(place[i] * height, 16), height)
            to = slice(i * height, (i + 1) * height)
            rows[to, :width] = dq[at, :]
            rows[to, width:] = dkv[at, :]

    total = sum(dot_nt(rows[:, c * width : (c + 1) * width], w_ref[c]) for c in range(3)).astype(BF)
    at = 0
    for out in outs:
        out[...] = total[at : at + out.shape[0]]
        at += out.shape[0]


def spread(place, dq, dkv, weight, start, columns, sizes, chunk=1024):
    total, width = dq.shape
    height = total // place.shape[0]
    skip = start // chunk
    return pl.pallas_call(
        functools.partial(spread_kernel, height),
        out_shape=tuple(jax.ShapeDtypeStruct((n * height, columns), BF) for n in sizes),
        grid_spec=pltpu.PrefetchScalarGridSpec(
            num_scalar_prefetch=1,
            grid=(columns // chunk,),
            in_specs=[
                pl.BlockSpec((total, width), lambda k, place: (0, 0)),
                pl.BlockSpec((total, 2 * width), lambda k, place: (0, 0)),
                pl.BlockSpec((3, chunk, width), lambda k, place: (0, k + skip, 0)),
            ],
            out_specs=tuple(pl.BlockSpec((n * height, chunk), lambda k, place: (0, k)) for n in sizes),
            scratch_shapes=[pltpu.VMEM((total, 3 * width), BF)],
        ),
        compiler_params=params(20),
        cost_estimate=cost(0.3),
        name="spread",
    )(place, dq, dkv, weight)


def body(hidden_states, qkv_weight, out_grad, tile_frame, frame_band):
    heads = frame_band.shape[0]
    width = qkv_weight.shape[2]
    head_dim = width // heads
    factor = 1.0 / math.sqrt(head_dim)
    scale2 = factor * math.log2(math.e)
    slabs, shards = lax.axis_size("slab"), lax.axis_size("head")
    slab, shard = lax.axis_index("slab"), lax.axis_index("head")
    height, model = hidden_states.shape
    part = model // 3
    slab_tiles = tile_frame.shape[0] // slabs

    def along_y(x, k):
        return lax.ppermute(x, "slab", [(i, (i + 4 * k) % slabs) for i in range(slabs)])

    def across_x(x):
        return lax.ppermute(x, "slab", [(i, i ^ 2) for i in range(slabs)])

    def across_core(x):
        return lax.ppermute(x, "slab", [(i, i ^ 1) for i in range(slabs)])

    def along_z(x, k):
        return lax.ppermute(x, "head", [(i, (i + 2 * k) % shards) for i in range(shards)])

    def across_far(x):
        return lax.ppermute(x, "head", [(i, i ^ 1) for i in range(shards)])

    z, far = shard // 2, shard % 2
    def places(shifts):
        return jnp.stack([((z + dz) % 4) * 2 + (far ^ dx) for dz, dx in shifts]).astype(jnp.int32)

    by_z = places([(dz, dx) for dz in STEPS for dx in (0, 1)])
    by_x = places([(dz, dx) for dx in (0, 1) for dz in STEPS])

    y, low = slab // 4, slab % 4
    frames = tile_frame.reshape(slabs, slab_tiles)
    query_frames = jnp.stack([frames[((y + d) % 4) * 4 + low] for d in STEPS])
    key_frames = jnp.concatenate([frames[y * 4 + (low ^ d)] for d in (0, 1, 2, 3)])
    distance = jnp.abs(query_frames[:, None, :] - key_frames[None, :, None])
    inside = distance[:, None] <= frame_band[None, :, None, None]
    bias = jnp.repeat(jnp.where(inside, 0.0, -FAR).astype(F32), TILE, axis=3)

    c, a, b = (hidden_states[:, i * part : (i + 1) * part] for i in range(3))
    up_c, down_c, two_c = along_z(c, 1), along_z(c, -1), along_z(c, 2)
    far_a = across_far(a)
    all_c = jnp.concatenate([c, up_c, down_c, two_c])
    far_c = across_far(all_c)
    pair_a = after(jnp.concatenate([a, far_a]), all_c)
    up_a, down_a = along_z(pair_a, 1), along_z(pair_a, -1)
    b = after(b, far_a, up_c)
    pair_b = jnp.concatenate([b, across_far(b)])
    down_b = along_z(pair_b, -1)
    up_b = along_z(after(pair_b, up_a), 1)
    two_a, two_b = along_z(up_a, 1), along_z(down_b, -1)
    grads = [out_grad, along_y(after(out_grad, up_c), 1)]
    grads.append(along_y(after(out_grad, grads[1]), -1))
    grads.append(along_y(after(out_grad, grads[2]), 2))

    streamed = pltpu.with_memory_space_constraint(qkv_weight, pltpu.HBM)
    acc = project(by_x, [all_c, far_c], streamed, 0)
    acc = project(by_z, [pair_a, up_a, down_a, two_a], qkv_weight, part, acc)
    acc, bias, grads[1:] = lax.optimization_barrier((acc, bias, grads[1:]))
    queries_own, pair_own = project(
        by_z, [pair_b, up_b, down_b, two_b], qkv_weight, 2 * part, acc, True
    )

    pair_x = across_x(pair_own)
    queries = [queries_own, along_y(queries_own, 1), along_y(queries_own, -1), along_y(queries_own, 2)]
    pair_x, queries[1:] = after((pair_x, queries[1:]), pair_own)
    pairs = [pair_own, across_core(pair_own), pair_x, across_core(pair_x)]

    out_t, stat = forward(scale2, queries, grads, pairs, bias)
    stats = [stat, along_y(stat, 1), along_y(stat, -1), along_y(stat, 2)]
    lse, delta = totals(stats)

    tiles = 2 * slab_tiles
    back = functools.partial(backward, scale2, factor)
    out_t = after(out_t, lse)
    outs = [out_t[0], along_y(out_t[2], 1), along_y(out_t[1], -1), along_y(out_t[3], 2)]
    dq, dx, dxc = back(queries, grads, pairs[2:], lse, delta, bias[:, :, tiles:])
    dq, dx, dxc, outs = lax.optimization_barrier((dq, dx, dxc, outs))
    dq, near = after((dq, dx + across_core(dxc)), dq)
    near = across_x(near)
    close = bias[:, :, :tiles]
    dqs, *sums = back(queries[1:], grads[1:], pairs[:2], lse, delta, close, 1, dq, None, False)
    got = [along_y(dqs[1], 1), along_y(dqs[0], -1), along_y(dqs[2], 2)]
    attn_out = merge(outs, stats)
    dq, near, attn_out = after((dq, near, attn_out), dqs)
    dq0, down_own, down_core = back(queries[:1], grads[:1], pairs[:2], lse, delta, close, 0, dq, sums)
    down_core, got = after((down_core, got), dq0)
    pair_grad = (
        down_own.astype(F32) + across_core(down_core).astype(F32) + near.astype(F32)
    ).astype(BF)
    query_grad = sum(x.astype(F32) for x in (dq0[0], *got)).astype(BF)

    send = functools.partial(spread, dkv=pair_grad, weight=qkv_weight, columns=part)
    own_a, prev_a, succ_a, out_a = send(by_z, query_grad, start=part, sizes=(2, 2, 2, 2))
    got_a, from_a = along_z(out_a, 1), along_z(prev_a, -1)
    own_c, prev_c, succ_c, out_c, other_c = send(
        by_x, after(query_grad, own_a), start=0, sizes=(1, 1, 1, 1, 4)
    )
    came_c = across_far(other_c)
    own_b, prev_b, succ_b, out_b = send(
        by_z, after(query_grad, own_c), start=2 * part, sizes=(2, 2, 2, 2)
    )
    got_b, from_b = along_z(out_b, -1), along_z(succ_b, 1)
    back_a = along_z(succ_a + got_a, 1)
    back_b = along_z(prev_b + got_b, -1)
    came_c = after(came_c, got_b)
    own_c, prev_c, succ_c, out_c = (
        (x.astype(F32) + came_c[i * height : (i + 1) * height].astype(F32)).astype(BF)
        for i, x in enumerate((own_c, prev_c, succ_c, out_c))
    )
    sums_c = (own_c, along_z(succ_c, 1), along_z(prev_c, -1), along_z(out_c, 2))
    done = [sum(x.astype(F32) for x in sums_c).astype(BF)]
    for own, one, other in ((own_a, from_a, back_a), (own_b, from_b, back_b)):
        total = own.astype(F32) + one.astype(F32) + other.astype(F32)
        rest = across_far(total[height:].astype(BF))
        done.append((total[:height] + rest.astype(F32)).astype(BF))
    return (attn_out, jnp.concatenate(done, axis=1))


def solution(mesh):
    placed = (P(("slab", "head"), None), P(None, None, "head"), P("slab", "head"), P(), P("head"))
    return jax.shard_map(
        body,
        mesh=mesh,
        in_specs=placed,
        out_specs=(P("slab", "head"), P(("slab", "head"), None)),
        check_vma=False,
    )
```

```python
import functools
import math

import jax
import jax.numpy as jnp
from jax import lax
from jax.experimental import pallas as pl
from jax.experimental.pallas import tpu as pltpu
from jax.sharding import PartitionSpec as P

TILE = 128
BF = jnp.bfloat16
F32 = jnp.float32
NT_DIMS = (((1,), (1,)), ((), ()))
FAR = 1e30
FROM = ((0, 1, 2, 3), (2, 0, 3, 1), (1, 3, 0, 2), (3, 2, 1, 0))
STEPS = (0, -1, 1, 2)


def params(mebibytes):
    return pltpu.CompilerParams(vmem_limit_bytes=mebibytes * 1024 * 1024)


def after(x, *others):
    return lax.optimization_barrier((x, others))[0]


def cost(micros):
    return pl.CostEstimate(flops=int(micros * 1.15e9), bytes_accessed=0, transcendentals=0)


def dot(a, b):
    return jnp.dot(a, b, preferred_element_type=F32)


def dot_nt(a, b):
    return lax.dot_general(a, b, NT_DIMS, preferred_element_type=F32)


def project_kernel(count, height, first, last, place, *refs):
    blocks, w_ref = refs[:count], refs[count]
    acc_in = None if first else refs[count + 1]
    outs, (rows, acc) = refs[count + (1 if first else 2) : -2], refs[-2:]
    step = pl.program_id(0)

    @pl.when(step == 0)
    def _():
        if first:
            acc[...] = jnp.zeros_like(acc)
        else:
            acc[...] = acc_in[...]

    i = 0
    for block in blocks:
        for r in range(0, block.shape[0], height):
            rows[pl.ds(pl.multiple_of(place[i] * height, 16), height), :] = block[r : r + height, :]
            i += 1
    side = dot(rows[...], jnp.concatenate([w_ref[c] for c in range(3)], axis=1))
    width = w_ref.shape[2]
    for c in range(3):
        acc[c] += side[:, c * width : (c + 1) * width]

    @pl.when(step == pl.num_programs(0) - 1)
    def _():
        if last:
            q_ref, kv_ref = outs
            q_ref[...] = acc[0].astype(BF)
            kv_ref[:, :width] = acc[1].astype(BF)
            kv_ref[:, width:] = acc[2].astype(BF)
        else:
            outs[0][...] = acc[...]


def project(place, blocks, weight, start, acc=None, last=False, chunk=1024):
    columns, width = blocks[0].shape[1], weight.shape[2]
    total = sum(b.shape[0] for b in blocks)
    height = total // place.shape[0]
    skip = start // chunk
    whole = pl.BlockSpec((3, total, width), lambda k, place: (0, 0, 0))
    if last:
        out_shape = (
            jax.ShapeDtypeStruct((total, width), BF),
            jax.ShapeDtypeStruct((total, 2 * width), BF),
        )
        out_specs = (
            pl.BlockSpec((total, width), lambda k, place: (0, 0)),
            pl.BlockSpec((total, 2 * width), lambda k, place: (0, 0)),
        )
    else:
        out_shape, out_specs = jax.ShapeDtypeStruct((3, total, width), F32), whole
    return pl.pallas_call(
        functools.partial(project_kernel, len(blocks), height, acc is None, last),
        out_shape=out_shape,
        grid_spec=pltpu.PrefetchScalarGridSpec(
            num_scalar_prefetch=1,
            grid=(columns // chunk,),
            in_specs=[pl.BlockSpec((b.shape[0], chunk), lambda k, place: (0, k)) for b in blocks]
            + [pl.BlockSpec((3, chunk, width), lambda k, place: (0, k + skip, 0))]
            + ([] if acc is None else [whole]),
            out_specs=out_specs,
            scratch_shapes=[pltpu.VMEM((total, chunk), BF), pltpu.VMEM((3, total, width), F32)],
        ),
        compiler_params=params(18),
        cost_estimate=cost(6),
        name="project",
    )(place, *blocks, weight, *([] if acc is None else [acc]))


def forward_kernel(scale2, q0, q1, q2, q3, g0, g1, g2, g3, kv0, kv1, kv2, kv3, bias, ot, stat, qs, gt, kv, vt):
    size, width = q0.shape
    heads = width // TILE
    for b, (q, g, k) in enumerate(((q0, g0, kv0), (q1, g1, kv1), (q2, g2, kv2), (q3, g3, kv3))):
        qs[b] = q[...]
        kv[b * size : (b + 1) * size, :] = k[:, :width]
        for h in range(heads):
            at = slice(h * TILE, (h + 1) * TILE)
            gt[b, h] = g[:, at].T
            vt[h, :, b * size : (b + 1) * size] = k[:, width + h * TILE : width + (h + 1) * TILE].T
    tiles = kv.shape[0] // TILE

    def step(b, carry):
        for h in range(heads):
            at = slice(h * TILE, (h + 1) * TILE)
            s = dot_nt(kv[:, at], qs[b, :, at])
            away = bias[b, h]
            peak = jnp.full((1, size), -FAR, F32)
            for t in range(tiles):
                top = jnp.max(s[t * TILE : (t + 1) * TILE], axis=0, keepdims=True) * scale2
                peak = jnp.maximum(peak, top + away[t : t + 1])
            total = jnp.zeros((1, size), F32)
            parts = []
            for t in range(tiles):
                base = jnp.where(away[t : t + 1] < 0, FAR, peak)
                p = jnp.exp2(s[t * TILE : (t + 1) * TILE] * scale2 - base)
                total = total + jnp.sum(p, axis=0, keepdims=True)
                parts.append(p.astype(BF))
            o = dot(vt[h], jnp.concatenate(parts, axis=0))
            stat[b, 3 * h : 3 * h + 1, :] = peak
            stat[b, 3 * h + 1 : 3 * h + 2, :] = total
            stat[b, 3 * h + 2 : 3 * h + 3, :] = jnp.sum(o * gt[b, h].astype(F32), axis=0, keepdims=True)
            ot[b, h] = (o * jnp.where(total > 0, 1.0 / total, 0.0)).astype(BF)
        return carry

    lax.fori_loop(0, 4, step, 0)


def forward(scale2, queries, grads, pairs, bias):
    size, width = queries[0].shape
    heads = width // TILE
    return pl.pallas_call(
        functools.partial(forward_kernel, scale2),
        out_shape=(
            jax.ShapeDtypeStruct((4, heads, TILE, size), BF),
            jax.ShapeDtypeStruct((4, 3 * heads, size), F32),
        ),
        scratch_shapes=[
            pltpu.VMEM((4, size, width), BF),
            pltpu.VMEM((4, heads, TILE, size), BF),
            pltpu.VMEM((4 * size, width), BF),
            pltpu.VMEM((heads, TILE, 4 * size), BF),
        ],
        compiler_params=params(24),
        cost_estimate=cost(17), name="forward",
    )(*queries, *grads, *pairs, bias)


def totals_kernel(s0, s1, s2, s3, lse_ref, delta_ref):
    heads = lse_ref.shape[1]
    sources = (s0, s1, s2, s3)
    for p in range(4):
        for h in range(heads):
            rows = [
                [s[FROM[j][p], 3 * h + i : 3 * h + i + 1, :] for i in range(3)]
                for j, s in enumerate(sources)
            ]
            peak = functools.reduce(jnp.maximum, [r[0] for r in rows])
            shrink = [jnp.exp2(r[0] - peak) for r in rows]
            total = sum(r[1] * f for r, f in zip(rows, shrink))
            lse_ref[p, h : h + 1, :] = peak + jnp.log2(total)
            delta_ref[p, h : h + 1, :] = sum(r[2] * f for r, f in zip(rows, shrink)) / total


def totals(stats):
    _, rows, size = stats[0].shape
    shape = jax.ShapeDtypeStruct((4, rows // 3, size), F32)
    return pl.pallas_call(totals_kernel, out_shape=(shape, shape), compiler_params=params(6), cost_estimate=cost(2), name="totals")(*stats)


def merge_kernel(o0, o1, o2, o3, s0, s1, s2, s3, out):
    heads = o0.shape[0]
    for h in range(heads):
        rows = [
            [s[FROM[j][0], 3 * h + i : 3 * h + i + 1, :] for i in range(2)]
            for j, s in enumerate((s0, s1, s2, s3))
        ]
        peak = functools.reduce(jnp.maximum, [r[0] for r in rows])
        shares = [r[1] * jnp.exp2(r[0] - peak) for r in rows]
        whole = sum(shares)
        o = sum(x[h].astype(F32) * (share / whole) for x, share in zip((o0, o1, o2, o3), shares))
        out[:, h * TILE : (h + 1) * TILE] = o.T.astype(BF)


def merge(outs, stats):
    heads, _, size = outs[0].shape
    return pl.pallas_call(
        merge_kernel,
        out_shape=jax.ShapeDtypeStruct((size, heads * TILE), BF),
        compiler_params=params(6),
        cost_estimate=cost(2), name="merge",
    )(*outs, *stats)


def backward_kernel(scale2, factor, count, chained, last, places, *refs):
    q_refs, refs = refs[:count], refs[count:]
    g_refs, refs = refs[:count], refs[count:]
    (kv_a, kv_b, lse, delta, bias), refs = refs[:5], refs[5:]
    if chained:
        (dq_in, dk_in, dv_in), refs = refs[:3], refs[3:]
    else:
        dq_in = dk_in = dv_in = None
    outs, (qs, gs, ks, vs, kt, dk, dv) = refs[:-7], refs[-7:]
    finish = dq_in is not None
    dq_out = outs[0]
    size, width = q_refs[0].shape
    heads = width // TILE
    for b in range(count):
        qs[b] = q_refs[b][...]
        gs[b] = g_refs[b][...]
    for i, k in enumerate((kv_a, kv_b)):
        ks[i * size : (i + 1) * size, :] = k[:, :width]
        vs[i * size : (i + 1) * size, :] = k[:, width:]
        for h in range(heads):
            kt[h, :, i * size : (i + 1) * size] = k[:, h * TILE : (h + 1) * TILE].T
    if dk_in is None:
        dk[...] = jnp.zeros_like(dk)
        dv[...] = jnp.zeros_like(dv)
    else:
        dk[...] = dk_in[...]
        dv[...] = dv_in[...]
    tiles = 2 * size // TILE

    def step(i, carry):
        b, h = i // heads, lax.rem(i, heads)
        p0 = places + b
        at = pl.ds(pl.multiple_of(h * TILE, TILE), TILE)
        q, g = qs[b, :, at], gs[b, :, at]
        s = dot_nt(ks[:, at], q)
        dp = dot_nt(vs[:, at], g)
        away, top, shift = bias[p0, h], lse[p0, pl.ds(h, 1)], delta[p0, pl.ds(h, 1)]
        probs, grads = [], []
        for t in range(tiles):
            rows = slice(t * TILE, (t + 1) * TILE)
            base = jnp.where(away[t : t + 1] < 0, FAR, top)
            p = jnp.exp2(s[rows] * scale2 - base)
            probs.append(p.astype(BF))
            grads.append((p * (dp[rows] - shift)).astype(BF))
        p = jnp.concatenate(probs, axis=0)
        ds = jnp.concatenate(grads, axis=0)
        dv[:, at] += dot(p, g)
        dk[:, at] += dot(ds, q)
        dq = dot(kt[h], ds)
        if finish:
            dq_out[b, :, at] = ((dq_in[p0, h] + dq) * factor).T.astype(BF)
        else:
            dq_out[b, h] = dq
        return carry

    lax.fori_loop(0, count * heads, step, 0)
    if last:
        for i, out in enumerate(outs[1:]):
            rows = slice(i * size, (i + 1) * size)
            out[:, :width] = (dk[rows] * factor).astype(BF)
            out[:, width:] = dv[rows].astype(BF)
    else:
        outs[1][...] = dk[...]
        outs[2][...] = dv[...]


def backward(scale2, factor, queries, grads, pairs, lse, delta, bias, places=0, dq=None, sums=None, last=True):
    size, width = queries[0].shape
    heads, count = width // TILE, len(queries)
    if last:
        tail = (jax.ShapeDtypeStruct((size, 2 * width), BF),) * 2
    else:
        tail = (jax.ShapeDtypeStruct((2 * size, width), F32),) * 2
    if dq is None:
        head = jax.ShapeDtypeStruct((count, heads, TILE, size), F32)
    else:
        head = jax.ShapeDtypeStruct((count, size, width), BF)
    chained = dq is not None
    extra = [dq, *sums] if sums is not None else ([dq] if chained else [])

    def kernel(*refs):
        refs = list(refs)
        if chained and sums is None:
            at = 2 * count + 6
            refs[at:at] = [None, None]
        backward_kernel(scale2, factor, count, chained, last, places, *refs)

    return pl.pallas_call(
        kernel,
        out_shape=(head, *tail),
        scratch_shapes=[
            pltpu.VMEM((count, size, width), BF),
            pltpu.VMEM((count, size, width), BF),
            pltpu.VMEM((2 * size, width), BF),
            pltpu.VMEM((2 * size, width), BF),
            pltpu.VMEM((heads, TILE, 2 * size), BF),
            pltpu.VMEM((2 * size, width), F32),
            pltpu.VMEM((2 * size, width), F32),
        ],
        compiler_params=params(26),
        cost_estimate=cost(4 * count), name="backward",
    )(*queries, *grads, *pairs, lse, delta, bias, *extra)


def spread_kernel(height, place, dq, dkv, w_ref, *refs):
    outs, rows = refs[:-1], refs[-1]
    width = dq.shape[1]

    @pl.when(pl.program_id(0) == 0)
    def _():
        for i in range(place.shape[0]):
            at = pl.ds(pl.multiple_of(place[i] * height, 16), height)
            to = slice(i * height, (i + 1) * height)
            rows[to, :width] = dq[at, :]
            rows[to, width:] = dkv[at, :]

    total = sum(dot_nt(rows[:, c * width : (c + 1) * width], w_ref[c]) for c in range(3)).astype(BF)
    at = 0
    for out in outs:
        out[...] = total[at : at + out.shape[0]]
        at += out.shape[0]


def spread(place, dq, dkv, weight, start, columns, sizes, chunk=1024):
    total, width = dq.shape
    height = total // place.shape[0]
    skip = start // chunk
    return pl.pallas_call(
        functools.partial(spread_kernel, height),
        out_shape=tuple(jax.ShapeDtypeStruct((n * height, columns), BF) for n in sizes),
        grid_spec=pltpu.PrefetchScalarGridSpec(
            num_scalar_prefetch=1,
            grid=(columns // chunk,),
            in_specs=[
                pl.BlockSpec((total, width), lambda k, place: (0, 0)),
                pl.BlockSpec((total, 2 * width), lambda k, place: (0, 0)),
                pl.BlockSpec((3, chunk, width), lambda k, place: (0, k + skip, 0)),
            ],
            out_specs=tuple(pl.BlockSpec((n * height, chunk), lambda k, place: (0, k)) for n in sizes),
            scratch_shapes=[pltpu.VMEM((total, 3 * width), BF)],
        ),
        compiler_params=params(20),
        cost_estimate=cost(0.3),
        name="spread",
    )(place, dq, dkv, weight)


def body(hidden_states, qkv_weight, out_grad, tile_frame, frame_band):
    heads = frame_band.shape[0]
    width = qkv_weight.shape[2]
    head_dim = width // heads
    factor = 1.0 / math.sqrt(head_dim)
    scale2 = factor * math.log2(math.e)
    slabs, shards = lax.axis_size("slab"), lax.axis_size("head")
    slab, shard = lax.axis_index("slab"), lax.axis_index("head")
    height, model = hidden_states.shape
    part = model // 3
    slab_tiles = tile_frame.shape[0] // slabs

    def along_y(x, k):
        return lax.ppermute(x, "slab", [(i, (i + 4 * k) % slabs) for i in range(slabs)])

    def across_x(x):
        return lax.ppermute(x, "slab", [(i, i ^ 2) for i in range(slabs)])

    def across_core(x):
        return lax.ppermute(x, "slab", [(i, i ^ 1) for i in range(slabs)])

    def along_z(x, k):
        return lax.ppermute(x, "head", [(i, (i + 2 * k) % shards) for i in range(shards)])

    def across_far(x):
        return lax.ppermute(x, "head", [(i, i ^ 1) for i in range(shards)])

    z, far = shard // 2, shard % 2
    def places(shifts):
        return jnp.stack([((z + dz) % 4) * 2 + (far ^ dx) for dz, dx in shifts]).astype(jnp.int32)

    by_z = places([(dz, dx) for dz in STEPS for dx in (0, 1)])
    by_x = places([(dz, dx) for dx in (0, 1) for dz in STEPS])

    y, low = slab // 4, slab % 4
    frames = tile_frame.reshape(slabs, slab_tiles)
    query_frames = jnp.stack([frames[((y + d) % 4) * 4 + low] for d in STEPS])
    key_frames = jnp.concatenate([frames[y * 4 + (low ^ d)] for d in (0, 1, 2, 3)])
    distance = jnp.abs(query_frames[:, None, :] - key_frames[None, :, None])
    inside = distance[:, None] <= frame_band[None, :, None, None]
    bias = jnp.repeat(jnp.where(inside, 0.0, -FAR).astype(F32), TILE, axis=3)

    c, a, b = (hidden_states[:, i * part : (i + 1) * part] for i in range(3))
    up_c, down_c, two_c = along_z(c, 1), along_z(c, -1), along_z(c, 2)
    far_a = across_far(a)
    all_c = jnp.concatenate([c, up_c, down_c, two_c])
    far_c = across_far(all_c)
    pair_a = after(jnp.concatenate([a, far_a]), all_c)
    up_a, down_a = along_z(pair_a, 1), along_z(pair_a, -1)
    b = after(b, far_a, up_c)
    pair_b = jnp.concatenate([b, across_far(b)])
    down_b = along_z(pair_b, -1)
    up_b = along_z(after(pair_b, up_a), 1)
    two_a, two_b = along_z(up_a, 1), along_z(down_b, -1)
    grads = [out_grad, along_y(after(out_grad, up_c), 1)]
    grads.append(along_y(after(out_grad, grads[1]), -1))
    grads.append(along_y(after(out_grad, grads[2]), 2))

    streamed = pltpu.with_memory_space_constraint(qkv_weight, pltpu.HBM)
    acc = project(by_x, [all_c, far_c], streamed, 0)
    acc = project(by_z, [pair_a, up_a, down_a, two_a], qkv_weight, part, acc)
    acc, bias, grads[1:] = lax.optimization_barrier((acc, bias, grads[1:]))
    queries_own, pair_own = project(
        by_z, [pair_b, up_b, down_b, two_b], qkv_weight, 2 * part, acc, True
    )

    pair_x = across_x(pair_own)
    queries = [queries_own, along_y(queries_own, 1), along_y(queries_own, -1), along_y(queries_own, 2)]
    pair_x, queries[1:] = after((pair_x, queries[1:]), pair_own)
    pairs = [pair_own, across_core(pair_own), pair_x, across_core(pair_x)]

    out_t, stat = forward(scale2, queries, grads, pairs, bias)
    stats = [stat, along_y(stat, 1), along_y(stat, -1), along_y(stat, 2)]
    lse, delta = totals(stats)

    tiles = 2 * slab_tiles
    back = functools.partial(backward, scale2, factor)
    out_t = after(out_t, lse)
    outs = [out_t[0], along_y(out_t[2], 1), along_y(out_t[1], -1), along_y(out_t[3], 2)]
    dq, dx, dxc = back(queries, grads, pairs[2:], lse, delta, bias[:, :, tiles:])
    dq, dx, dxc, outs = lax.optimization_barrier((dq, dx, dxc, outs))
    dq, near = after((dq, dx + across_core(dxc)), dq)
    near = across_x(near)
    close = bias[:, :, :tiles]
    dqs, *sums = back(queries[1:], grads[1:], pairs[:2], lse, delta, close, 1, dq, None, False)
    got = [along_y(dqs[1], 1), along_y(dqs[0], -1), along_y(dqs[2], 2)]
    attn_out = merge(outs, stats)
    dq, near, attn_out = after((dq, near, attn_out), dqs)
    dq0, down_own, down_core = back(queries[:1], grads[:1], pairs[:2], lse, delta, close, 0, dq, sums)
    down_core, got = after((down_core, got), dq0)
    pair_grad = (
        down_own.astype(F32) + across_core(down_core).astype(F32) + near.astype(F32)
    ).astype(BF)
    query_grad = sum(x.astype(F32) for x in (dq0[0], *got)).astype(BF)

    send = functools.partial(spread, dkv=pair_grad, weight=qkv_weight, columns=part)
    own_a, prev_a, succ_a, out_a = send(by_z, query_grad, start=part, sizes=(2, 2, 2, 2))
    got_a, from_a = along_z(out_a, 1), along_z(prev_a, -1)
    own_c, prev_c, succ_c, out_c, other_c = send(
        by_x, after(query_grad, own_a), start=0, sizes=(1, 1, 1, 1, 4)
    )
    came_c = across_far(other_c)
    own_b, prev_b, succ_b, out_b = send(
        by_z, after(query_grad, own_c), start=2 * part, sizes=(2, 2, 2, 2)
    )
    got_b, from_b = along_z(out_b, -1), along_z(succ_b, 1)
    back_a = along_z(succ_a + got_a, 1)
    back_b = along_z(prev_b + got_b, -1)
    came_c = after(came_c, got_b)
    own_c, prev_c, succ_c, out_c = (
        (x.astype(F32) + came_c[i * height : (i + 1) * height].astype(F32)).astype(BF)
        for i, x in enumerate((own_c, prev_c, succ_c, out_c))
    )
    sums_c = (own_c, along_z(succ_c, 1), along_z(prev_c, -1), along_z(out_c, 2))
    done = [sum(x.astype(F32) for x in sums_c).astype(BF)]
    for own, one, other in ((own_a, from_a, back_a), (own_b, from_b, back_b)):
        total = own.astype(F32) + one.astype(F32) + other.astype(F32)
        rest = across_far(total[height:].astype(BF))
        done.append((total[:height] + rest.astype(F32)).astype(BF))
    return (attn_out, jnp.concatenate(done, axis=1))


def solution(mesh):
    placed = (P(("slab", "head"), None), P(None, None, "head"), P("slab", "head"), P(), P("head"))
    return jax.shard_map(
        body,
        mesh=mesh,
        in_specs=placed,
        out_specs=(P("slab", "head"), P(("slab", "head"), None)),
        check_vma=False,
    )
```

```python
import functools
import math

import jax
import jax.numpy as jnp
from jax import lax
from jax.experimental import pallas as pl
from jax.experimental.pallas import tpu as pltpu
from jax.sharding import PartitionSpec as P

TILE = 128
BF = jnp.bfloat16
F32 = jnp.float32
NT_DIMS = (((1,), (1,)), ((), ()))
FAR = 1e30
FROM = ((0, 1, 2, 3), (2, 0, 3, 1), (1, 3, 0, 2), (3, 2, 1, 0))
STEPS = (0, -1, 1, 2)


def params(mebibytes):
    return pltpu.CompilerParams(vmem_limit_bytes=mebibytes * 1024 * 1024)


def after(x, *others):
    return lax.optimization_barrier((x, others))[0]


def cost(micros):
    return pl.CostEstimate(flops=int(micros * 1.15e9), bytes_accessed=0, transcendentals=0)


def dot(a, b):
    return jnp.dot(a, b, preferred_element_type=F32)


def dot_nt(a, b):
    return lax.dot_general(a, b, NT_DIMS, preferred_element_type=F32)


def project_kernel(count, height, first, last, place, *refs):
    blocks, w_ref = refs[:count], refs[count]
    acc_in = None if first else refs[count + 1]
    outs, (rows, acc) = refs[count + (1 if first else 2) : -2], refs[-2:]
    step = pl.program_id(0)

    @pl.when(step == 0)
    def _():
        if first:
            acc[...] = jnp.zeros_like(acc)
        else:
            acc[...] = acc_in[...]

    i = 0
    for block in blocks:
        for r in range(0, block.shape[0], height):
            rows[pl.ds(pl.multiple_of(place[i] * height, 16), height), :] = block[r : r + height, :]
            i += 1
    side = dot(rows[...], jnp.concatenate([w_ref[c] for c in range(3)], axis=1))
    width = w_ref.shape[2]
    for c in range(3):
        acc[c] += side[:, c * width : (c + 1) * width]

    @pl.when(step == pl.num_programs(0) - 1)
    def _():
        if last:
            q_ref, kv_ref = outs
            q_ref[...] = acc[0].astype(BF)
            kv_ref[:, :width] = acc[1].astype(BF)
            kv_ref[:, width:] = acc[2].astype(BF)
        else:
            outs[0][...] = acc[...]


def project(place, blocks, weight, start, acc=None, last=False, chunk=1024):
    columns, width = blocks[0].shape[1], weight.shape[2]
    total = sum(b.shape[0] for b in blocks)
    height = total // place.shape[0]
    skip = start // chunk
    whole = pl.BlockSpec((3, total, width), lambda k, place: (0, 0, 0))
    if last:
        out_shape = (
            jax.ShapeDtypeStruct((total, width), BF),
            jax.ShapeDtypeStruct((total, 2 * width), BF),
        )
        out_specs = (
            pl.BlockSpec((total, width), lambda k, place: (0, 0)),
            pl.BlockSpec((total, 2 * width), lambda k, place: (0, 0)),
        )
    else:
        out_shape, out_specs = jax.ShapeDtypeStruct((3, total, width), F32), whole
    return pl.pallas_call(
        functools.partial(project_kernel, len(blocks), height, acc is None, last),
        out_shape=out_shape,
        grid_spec=pltpu.PrefetchScalarGridSpec(
            num_scalar_prefetch=1,
            grid=(columns // chunk,),
            in_specs=[pl.BlockSpec((b.shape[0], chunk), lambda k, place: (0, k)) for b in blocks]
            + [pl.BlockSpec((3, chunk, width), lambda k, place: (0, k + skip, 0))]
            + ([] if acc is None else [whole]),
            out_specs=out_specs,
            scratch_shapes=[pltpu.VMEM((total, chunk), BF), pltpu.VMEM((3, total, width), F32)],
        ),
        compiler_params=params(18),
        cost_estimate=cost(6),
        name="project",
    )(place, *blocks, weight, *([] if acc is None else [acc]))


def forward_kernel(scale2, q0, q1, q2, q3, g0, g1, g2, g3, kv0, kv1, kv2, kv3, bias, ot, stat, qs, gt, kv, vt):
    size, width = q0.shape
    heads = width // TILE
    for b, (q, g, k) in enumerate(((q0, g0, kv0), (q1, g1, kv1), (q2, g2, kv2), (q3, g3, kv3))):
        qs[b] = q[...]
        kv[b * size : (b + 1) * size, :] = k[:, :width]
        for h in range(heads):
            at = slice(h * TILE, (h + 1) * TILE)
            gt[b, h] = g[:, at].T
            vt[h, :, b * size : (b + 1) * size] = k[:, width + h * TILE : width + (h + 1) * TILE].T
    tiles = kv.shape[0] // TILE

    def step(b, carry):
        for h in range(heads):
            at = slice(h * TILE, (h + 1) * TILE)
            s = dot_nt(kv[:, at], qs[b, :, at])
            away = bias[b, h]
            peak = jnp.full((1, size), -FAR, F32)
            for t in range(tiles):
                top = jnp.max(s[t * TILE : (t + 1) * TILE], axis=0, keepdims=True) * scale2
                peak = jnp.maximum(peak, top + away[t : t + 1])
            total = jnp.zeros((1, size), F32)
            parts = []
            for t in range(tiles):
                base = jnp.where(away[t : t + 1] < 0, FAR, peak)
                p = jnp.exp2(s[t * TILE : (t + 1) * TILE] * scale2 - base)
                total = total + jnp.sum(p, axis=0, keepdims=True)
                parts.append(p.astype(BF))
            o = dot(vt[h], jnp.concatenate(parts, axis=0))
            stat[b, 3 * h : 3 * h + 1, :] = peak
            stat[b, 3 * h + 1 : 3 * h + 2, :] = total
            stat[b, 3 * h + 2 : 3 * h + 3, :] = jnp.sum(o * gt[b, h].astype(F32), axis=0, keepdims=True)
            ot[b, h] = (o * jnp.where(total > 0, 1.0 / total, 0.0)).astype(BF)
        return carry

    lax.fori_loop(0, 4, step, 0)


def forward(scale2, queries, grads, pairs, bias):
    size, width = queries[0].shape
    heads = width // TILE
    return pl.pallas_call(
        functools.partial(forward_kernel, scale2),
        out_shape=(
            jax.ShapeDtypeStruct((4, heads, TILE, size), BF),
            jax.ShapeDtypeStruct((4, 3 * heads, size), F32),
        ),
        scratch_shapes=[
            pltpu.VMEM((4, size, width), BF),
            pltpu.VMEM((4, heads, TILE, size), BF),
            pltpu.VMEM((4 * size, width), BF),
            pltpu.VMEM((heads, TILE, 4 * size), BF),
        ],
        compiler_params=params(24),
        cost_estimate=cost(17), name="forward",
    )(*queries, *grads, *pairs, bias)


def totals_kernel(s0, s1, s2, s3, lse_ref, delta_ref):
    heads = lse_ref.shape[1]
    sources = (s0, s1, s2, s3)
    for p in range(4):
        for h in range(heads):
            rows = [
                [s[FROM[j][p], 3 * h + i : 3 * h + i + 1, :] for i in range(3)]
                for j, s in enumerate(sources)
            ]
            peak = functools.reduce(jnp.maximum, [r[0] for r in rows])
            shrink = [jnp.exp2(r[0] - peak) for r in rows]
            total = sum(r[1] * f for r, f in zip(rows, shrink))
            lse_ref[p, h : h + 1, :] = peak + jnp.log2(total)
            delta_ref[p, h : h + 1, :] = sum(r[2] * f for r, f in zip(rows, shrink)) / total


def totals(stats):
    _, rows, size = stats[0].shape
    shape = jax.ShapeDtypeStruct((4, rows // 3, size), F32)
    return pl.pallas_call(totals_kernel, out_shape=(shape, shape), compiler_params=params(6), cost_estimate=cost(2), name="totals")(*stats)


def merge_kernel(o0, o1, o2, o3, s0, s1, s2, s3, out):
    heads = o0.shape[0]
    for h in range(heads):
        rows = [
            [s[FROM[j][0], 3 * h + i : 3 * h + i + 1, :] for i in range(2)]
            for j, s in enumerate((s0, s1, s2, s3))
        ]
        peak = functools.reduce(jnp.maximum, [r[0] for r in rows])
        shares = [r[1] * jnp.exp2(r[0] - peak) for r in rows]
        whole = sum(shares)
        o = sum(x[h].astype(F32) * (share / whole) for x, share in zip((o0, o1, o2, o3), shares))
        out[:, h * TILE : (h + 1) * TILE] = o.T.astype(BF)


def merge(outs, stats):
    heads, _, size = outs[0].shape
    return pl.pallas_call(
        merge_kernel,
        out_shape=jax.ShapeDtypeStruct((size, heads * TILE), BF),
        compiler_params=params(6),
        cost_estimate=cost(2), name="merge",
    )(*outs, *stats)


def backward_kernel(scale2, factor, count, chained, last, places, *refs):
    q_refs, refs = refs[:count], refs[count:]
    g_refs, refs = refs[:count], refs[count:]
    (kv_a, kv_b, lse, delta, bias), refs = refs[:5], refs[5:]
    if chained:
        (dq_in, dk_in, dv_in), refs = refs[:3], refs[3:]
    else:
        dq_in = dk_in = dv_in = None
    outs, (qs, gs, ks, vs, kt, dk, dv) = refs[:-7], refs[-7:]
    finish = dq_in is not None
    dq_out = outs[0]
    size, width = q_refs[0].shape
    heads = width // TILE
    for b in range(count):
        qs[b] = q_refs[b][...]
        gs[b] = g_refs[b][...]
    for i, k in enumerate((kv_a, kv_b)):
        ks[i * size : (i + 1) * size, :] = k[:, :width]
        vs[i * size : (i + 1) * size, :] = k[:, width:]
        for h in range(heads):
            kt[h, :, i * size : (i + 1) * size] = k[:, h * TILE : (h + 1) * TILE].T
    if dk_in is None:
        dk[...] = jnp.zeros_like(dk)
        dv[...] = jnp.zeros_like(dv)
    else:
        dk[...] = dk_in[...]
        dv[...] = dv_in[...]
    tiles = 2 * size // TILE

    def step(i, carry):
        b, h = i // heads, lax.rem(i, heads)
        p0 = places + b
        at = pl.ds(pl.multiple_of(h * TILE, TILE), TILE)
        q, g = qs[b, :, at], gs[b, :, at]
        s = dot_nt(ks[:, at], q)
        dp = dot_nt(vs[:, at], g)
        away, top, shift = bias[p0, h], lse[p0, pl.ds(h, 1)], delta[p0, pl.ds(h, 1)]
        probs, grads = [], []
        for t in range(tiles):
            rows = slice(t * TILE, (t + 1) * TILE)
            base = jnp.where(away[t : t + 1] < 0, FAR, top)
            p = jnp.exp2(s[rows] * scale2 - base)
            probs.append(p.astype(BF))
            grads.append((p * (dp[rows] - shift)).astype(BF))
        p = jnp.concatenate(probs, axis=0)
        ds = jnp.concatenate(grads, axis=0)
        dv[:, at] += dot(p, g)
        dk[:, at] += dot(ds, q)
        dq = dot(kt[h], ds)
        if finish:
            dq_out[b, :, at] = ((dq_in[p0, h] + dq) * factor).T.astype(BF)
        else:
            dq_out[b, h] = dq
        return carry

    lax.fori_loop(0, count * heads, step, 0)
    if last:
        for i, out in enumerate(outs[1:]):
            rows = slice(i * size, (i + 1) * size)
            out[:, :width] = (dk[rows] * factor).astype(BF)
            out[:, width:] = dv[rows].astype(BF)
    else:
        outs[1][...] = dk[...]
        outs[2][...] = dv[...]


def backward(scale2, factor, queries, grads, pairs, lse, delta, bias, places=0, dq=None, sums=None, last=True):
    size, width = queries[0].shape
    heads, count = width // TILE, len(queries)
    if last:
        tail = (jax.ShapeDtypeStruct((size, 2 * width), BF),) * 2
    else:
        tail = (jax.ShapeDtypeStruct((2 * size, width), F32),) * 2
    if dq is None:
        head = jax.ShapeDtypeStruct((count, heads, TILE, size), F32)
    else:
        head = jax.ShapeDtypeStruct((count, size, width), BF)
    chained = dq is not None
    extra = [dq, *sums] if sums is not None else ([dq] if chained else [])

    def kernel(*refs):
        refs = list(refs)
        if chained and sums is None:
            at = 2 * count + 6
            refs[at:at] = [None, None]
        backward_kernel(scale2, factor, count, chained, last, places, *refs)

    return pl.pallas_call(
        kernel,
        out_shape=(head, *tail),
        scratch_shapes=[
            pltpu.VMEM((count, size, width), BF),
            pltpu.VMEM((count, size, width), BF),
            pltpu.VMEM((2 * size, width), BF),
            pltpu.VMEM((2 * size, width), BF),
            pltpu.VMEM((heads, TILE, 2 * size), BF),
            pltpu.VMEM((2 * size, width), F32),
            pltpu.VMEM((2 * size, width), F32),
        ],
        compiler_params=params(26),
        cost_estimate=cost(4 * count), name="backward",
    )(*queries, *grads, *pairs, lse, delta, bias, *extra)


def spread_kernel(height, place, dq, dkv, w_ref, *refs):
    outs, rows = refs[:-1], refs[-1]
    width = dq.shape[1]

    @pl.when(pl.program_id(0) == 0)
    def _():
        for i in range(place.shape[0]):
            at = pl.ds(pl.multiple_of(place[i] * height, 16), height)
            to = slice(i * height, (i + 1) * height)
            rows[to, :width] = dq[at, :]
            rows[to, width:] = dkv[at, :]

    total = sum(dot_nt(rows[:, c * width : (c + 1) * width], w_ref[c]) for c in range(3)).astype(BF)
    at = 0
    for out in outs:
        out[...] = total[at : at + out.shape[0]]
        at += out.shape[0]


def spread(place, dq, dkv, weight, start, columns, sizes, chunk=1024):
    total, width = dq.shape
    height = total // place.shape[0]
    skip = start // chunk
    return pl.pallas_call(
        functools.partial(spread_kernel, height),
        out_shape=tuple(jax.ShapeDtypeStruct((n * height, columns), BF) for n in sizes),
        grid_spec=pltpu.PrefetchScalarGridSpec(
            num_scalar_prefetch=1,
            grid=(columns // chunk,),
            in_specs=[
                pl.BlockSpec((total, width), lambda k, place: (0, 0)),
                pl.BlockSpec((total, 2 * width), lambda k, place: (0, 0)),
                pl.BlockSpec((3, chunk, width), lambda k, place: (0, k + skip, 0)),
            ],
            out_specs=tuple(pl.BlockSpec((n * height, chunk), lambda k, place: (0, k)) for n in sizes),
            scratch_shapes=[pltpu.VMEM((total, 3 * width), BF)],
        ),
        compiler_params=params(20),
        cost_estimate=cost(0.3),
        name="spread",
    )(place, dq, dkv, weight)


def body(hidden_states, qkv_weight, out_grad, tile_frame, frame_band):
    heads = frame_band.shape[0]
    width = qkv_weight.shape[2]
    head_dim = width // heads
    factor = 1.0 / math.sqrt(head_dim)
    scale2 = factor * math.log2(math.e)
    slabs, shards = lax.axis_size("slab"), lax.axis_size("head")
    slab, shard = lax.axis_index("slab"), lax.axis_index("head")
    height, model = hidden_states.shape
    part = model // 3
    slab_tiles = tile_frame.shape[0] // slabs

    def along_y(x, k):
        return lax.ppermute(x, "slab", [(i, (i + 4 * k) % slabs) for i in range(slabs)])

    def across_x(x):
        return lax.ppermute(x, "slab", [(i, i ^ 2) for i in range(slabs)])

    def across_core(x):
        return lax.ppermute(x, "slab", [(i, i ^ 1) for i in range(slabs)])

    def along_z(x, k):
        return lax.ppermute(x, "head", [(i, (i + 2 * k) % shards) for i in range(shards)])

    def across_far(x):
        return lax.ppermute(x, "head", [(i, i ^ 1) for i in range(shards)])

    z, far = shard // 2, shard % 2
    def places(shifts):
        return jnp.stack([((z + dz) % 4) * 2 + (far ^ dx) for dz, dx in shifts]).astype(jnp.int32)

    by_z = places([(dz, dx) for dz in STEPS for dx in (0, 1)])
    by_x = places([(dz, dx) for dx in (0, 1) for dz in STEPS])

    y, low = slab // 4, slab % 4
    frames = tile_frame.reshape(slabs, slab_tiles)
    query_frames = jnp.stack([frames[((y + d) % 4) * 4 + low] for d in STEPS])
    key_frames = jnp.concatenate([frames[y * 4 + (low ^ d)] for d in (0, 1, 2, 3)])
    distance = jnp.abs(query_frames[:, None, :] - key_frames[None, :, None])
    inside = distance[:, None] <= frame_band[None, :, None, None]
    bias = jnp.repeat(jnp.where(inside, 0.0, -FAR).astype(F32), TILE, axis=3)

    c, a, b = (hidden_states[:, i * part : (i + 1) * part] for i in range(3))
    up_c, down_c, two_c = along_z(c, 1), along_z(c, -1), along_z(c, 2)
    far_a = across_far(a)
    all_c = jnp.concatenate([c, up_c, down_c, two_c])
    far_c = across_far(all_c)
    pair_a = after(jnp.concatenate([a, far_a]), all_c)
    up_a, down_a = along_z(pair_a, 1), along_z(pair_a, -1)
    b = after(b, far_a, up_c)
    pair_b = jnp.concatenate([b, across_far(b)])
    down_b = along_z(pair_b, -1)
    up_b = along_z(after(pair_b, far_c), 1)
    two_a, two_b = along_z(up_a, 1), along_z(down_b, -1)
    grads = [out_grad, along_y(after(out_grad, up_c), 1)]
    grads.append(along_y(after(out_grad, grads[1]), -1))
    grads.append(along_y(after(out_grad, grads[2]), 2))

    streamed = pltpu.with_memory_space_constraint(qkv_weight, pltpu.HBM)
    acc = project(by_x, [all_c, far_c], streamed, 0)
    acc = project(by_z, [pair_a, up_a, down_a, two_a], qkv_weight, part, acc)
    acc, bias, grads[1:] = lax.optimization_barrier((acc, bias, grads[1:]))
    queries_own, pair_own = project(
        by_z, [pair_b, up_b, down_b, two_b], qkv_weight, 2 * part, acc, True
    )

    pair_x = across_x(pair_own)
    queries = [queries_own, along_y(queries_own, 1), along_y(queries_own, -1), along_y(queries_own, 2)]
    pair_x, queries[1:] = after((pair_x, queries[1:]), pair_own)
    pairs = [pair_own, across_core(pair_own), pair_x, across_core(pair_x)]

    out_t, stat = forward(scale2, queries, grads, pairs, bias)
    stats = [stat, along_y(stat, 1), along_y(stat, -1), along_y(stat, 2)]
    lse, delta = totals(stats)

    tiles = 2 * slab_tiles
    back = functools.partial(backward, scale2, factor)
    out_t = after(out_t, lse)
    outs = [out_t[0], along_y(out_t[2], 1), along_y(out_t[1], -1), along_y(out_t[3], 2)]
    dq, dx, dxc = back(queries, grads, pairs[2:], lse, delta, bias[:, :, tiles:])
    dq, dx, dxc, outs = lax.optimization_barrier((dq, dx, dxc, outs))
    dq, near = after((dq, dx + across_core(dxc)), dq)
    near = across_x(near)
    close = bias[:, :, :tiles]
    dqs, *sums = back(queries[1:], grads[1:], pairs[:2], lse, delta, close, 1, dq, None, False)
    got = [along_y(dqs[1], 1), along_y(dqs[0], -1), along_y(dqs[2], 2)]
    attn_out = merge(outs, stats)
    dq, near, attn_out = after((dq, near, attn_out), dqs)
    dq0, down_own, down_core = back(queries[:1], grads[:1], pairs[:2], lse, delta, close, 0, dq, sums)
    down_core, got = after((down_core, got), dq0)
    pair_grad = (
        down_own.astype(F32) + across_core(down_core).astype(F32) + near.astype(F32)
    ).astype(BF)
    query_grad = sum(x.astype(F32) for x in (dq0[0], *got)).astype(BF)

    send = functools.partial(spread, dkv=pair_grad, weight=qkv_weight, columns=part)
    own_a, prev_a, succ_a, out_a = send(by_z, query_grad, start=part, sizes=(2, 2, 2, 2))
    got_a, from_a = along_z(out_a, 1), along_z(prev_a, -1)
    own_c, prev_c, succ_c, out_c, other_c = send(
        by_x, after(query_grad, own_a), start=0, sizes=(1, 1, 1, 1, 4)
    )
    came_c = across_far(other_c)
    own_b, prev_b, succ_b, out_b = send(
        by_z, after(query_grad, own_c), start=2 * part, sizes=(2, 2, 2, 2)
    )
    got_b, from_b = along_z(out_b, -1), along_z(succ_b, 1)
    back_a = along_z(succ_a + got_a, 1)
    back_b = along_z(prev_b + got_b, -1)
    came_c = after(came_c, got_b)
    own_c, prev_c, succ_c, out_c = (
        (x.astype(F32) + came_c[i * height : (i + 1) * height].astype(F32)).astype(BF)
        for i, x in enumerate((own_c, prev_c, succ_c, out_c))
    )
    sums_c = (own_c, along_z(succ_c, 1), along_z(prev_c, -1), along_z(out_c, 2))
    done = [sum(x.astype(F32) for x in sums_c).astype(BF)]
    for own, one, other in ((own_a, from_a, back_a), (own_b, from_b, back_b)):
        total = own.astype(F32) + one.astype(F32) + other.astype(F32)
        rest = across_far(total[height:].astype(BF))
        done.append((total[:height] + rest.astype(F32)).astype(BF))
    return (attn_out, jnp.concatenate(done, axis=1))


def solution(mesh):
    placed = (P(("slab", "head"), None), P(None, None, "head"), P("slab", "head"), P(), P("head"))
    return jax.shard_map(
        body,
        mesh=mesh,
        in_specs=placed,
        out_specs=(P("slab", "head"), P(("slab", "head"), None)),
        check_vma=False,
    )
```
